32 devices in a mesh: grp: 2 (over x), slc: 16 (over z, y, core).
Axes of the slice: x: 2, y: 2, z: 4, core: 2. Of those that a mesh axis runs over, the one named last changes fastest.
Arguments:
- kspace: bfloat16 [4, 32, 16, 16384], P('grp', None, None, 'slc'), parts along dimension 0, may hold values from -6 to 6
- coil_maps: bfloat16 [4, 32, 16, 128, 128], P('grp', 'slc'), parts along dimension 0, may hold values from -1 to 1, as said below
- sample_mask: int32 [64, 16, 128], P('grp'), parts along dimension 0, may hold values 0 or 1
- tap_order: int32 [27], replicated, may hold values from 0 to 26, each once
- first_kernel: bfloat16 [27, 2, 64], replicated, may hold values from -0.875 to 0.875
- first_bias: float32 [64], replicated, may hold values from -2 to 2
- second_kernel: bfloat16 [27, 64, 2], replicated, may hold values from -0.15625 to 0.15625
- second_bias: float32 [2], replicated, may hold values from -2 to 2
Outputs:
- estimate: float32 [4, 32, 128, 128], P('grp', 'slc'), parts along dimension 0
- dual_var: float32 [4, 32, 128, 128], P('grp', 'slc'), parts along dimension 0
The draws below stay inside these ranges and needn't reach their ends.
There are 2 independent parts, one for each index of `grp`. The reference program is written for one: setup_inputs(seed, part) draws one part's arguments, and reference() takes and returns one part's arrays. A program takes and returns all parts, laid end to end along the dimension named above; an argument that names none is the same for every part. Nothing has to cross between parts.
Inputs may be any that keep to these rules, and one draw needn't show every extreme that they name: `coil_maps`: at every cell the squared real and imaginary parts of the maps summed over the 16 coils make one, up to rounding. `tap_order`: each tap index appears exactly once.
All inputs are finite; a program needn't handle non-finite values.
Results may differ from the reference program's by a relative error of at most 0.014.
Values may be sent and summed in bfloat16 or wider, within the bound.
No kernel may reach another device: no remote copies, remote signals or barrier semaphores. Data moves between devices by JAX's collectives and lax.ppermute only.
A program may use at most 128 MiB of HBM per device.

```python
import math
import jax
import jax.numpy as jnp
from jax import lax

C = 16
H = 128
W = 128
HID = 64
ITERS = 1
S = 32


def draw_coil_maps(key, part):
    shape = (2, S, C, H, W)
    samples = jax.random.normal(key, shape, jnp.float32)
    energy = jnp.sum(samples * samples, axis=(0, 2), keepdims=True)
    return (samples / jnp.sqrt(energy + 1e-06)).astype(jnp.bfloat16)


def touch_ends(array, rng, low, high):
    longest = array.shape.index(max(array.shape))
    spots = []
    for shift in (0, 1):
        where = [jax.random.randint(jax.random.fold_in(rng, axis), (), 0, length) for axis, length in enumerate(array.shape)]
        where[longest] = (where[longest] + shift) % array.shape[longest]
        spots.append(tuple(where))
    return array.at[spots[0]].set(low).at[spots[1]].set(high)


def shard_levels(key, extent, pieces, smallest, largest):
    level, own = 1.0, jax.random.fold_in(key, 6)
    for position, parts in pieces:
        draws = jnp.exp(jax.random.uniform(jax.random.fold_in(own, position), (parts,), jnp.float32, smallest / len(pieces), largest / len(pieces)))
        level = level * jnp.repeat(draws, extent[position] // parts).reshape([-1 if axis == position else 1 for axis in range(len(extent))])
    return level


def normal_values(rng, extent, spread, bound, split=(), kind=jnp.bfloat16):
    drawn = spread * jax.random.normal(rng, extent, jnp.float32)
    if split:
        drawn = drawn * shard_levels(rng, extent, split, -0.22, 0.18)
    return jnp.clip(drawn, -bound, bound).astype(kind)


def setup_inputs(seed: int = 0, part: int = 0) -> dict:
    splits = jax.random.split(jax.random.key(seed), 9)
    part_keys = jax.random.split(jax.random.fold_in(splits[8], part), 9)
    return {
        "kspace": normal_values(part_keys[0], (2, S, C, H * W), 1.0, 6.0, ((3, 16),)),
        "coil_maps": draw_coil_maps(jax.random.fold_in(jax.random.fold_in(splits[8], part), 71), part),
        "sample_mask": touch_ends((jax.random.randint(part_keys[2], (S, C, H), 0, 6) < 5).astype(jnp.int32), jax.random.fold_in(part_keys[2], 1), 0, 1),
        "tap_order": jax.random.permutation(splits[3], 27).astype(jnp.int32),
        "first_kernel": normal_values(splits[4], (27, 2, HID), 54 ** -0.5, 0.875),
        "first_bias": normal_values(splits[5], (HID,), 0.5, 2.0, (), jnp.float32),
        "second_kernel": normal_values(splits[6], (27, HID, 2), (27 * HID) ** -0.5, 0.15625),
        "second_bias": normal_values(splits[7], (2,), 0.5, 2.0, (), jnp.float32),
    }


def make_table(length, direction):
    positions = jnp.arange(length, dtype=jnp.int32)
    product = positions[:, None] * positions[None, :] % length
    angles = 2.0 * math.pi / length * product.astype(jnp.float32)
    norm_scale = 1.0 / math.sqrt(length)
    real_part = (jnp.cos(angles) * norm_scale).astype(jnp.bfloat16)
    imaginary = (direction * jnp.sin(angles) * norm_scale).astype(jnp.bfloat16)
    return (real_part, imaginary)

def transform(pattern, matrix, values):
    highest = lax.Precision.HIGHEST
    matrix_real = matrix[0].astype(jnp.float32)
    matrix_imag = matrix[1].astype(jnp.float32)
    value_real = values[0].astype(jnp.float32)
    value_imag = values[1].astype(jnp.float32)
    real_out = jnp.einsum(pattern, value_real, matrix_real, precision=highest) - jnp.einsum(pattern, value_imag, matrix_imag, precision=highest)
    imag_out = jnp.einsum(pattern, value_real, matrix_imag, precision=highest) + jnp.einsum(pattern, value_imag, matrix_real, precision=highest)
    return jnp.stack([real_out, imag_out])

def coil_forward(image, coil_map, tables):
    map_real = coil_map[0].astype(jnp.float32)
    map_imag = coil_map[1].astype(jnp.float32)
    coil_image = jnp.stack([map_real * image[0] - map_imag * image[1], map_real * image[1] + map_imag * image[0]]).astype(jnp.bfloat16)
    row_done = transform('zyj,kj->zyk', tables[0], coil_image).astype(jnp.bfloat16)
    plane = transform('zjx,kj->zkx', tables[1], row_done).astype(jnp.bfloat16)
    return transform('jyx,kj->kyx', tables[2], plane)

def coil_adjoint(residual, coil_map, tables):
    depth_back = transform('jyx,kj->kyx', tables[5], residual).astype(jnp.bfloat16)
    upward = transform('zjx,kj->zkx', tables[4], depth_back).astype(jnp.bfloat16)
    image_back = transform('zyj,kj->zyk', tables[3], upward)
    map_real = coil_map[0].astype(jnp.float32)
    map_imag = coil_map[1].astype(jnp.float32)
    return jnp.stack([map_real * image_back[0] + map_imag * image_back[1], map_real * image_back[1] - map_imag * image_back[0]])

def tap_kernel(tap_order, stored):
    chosen = (tap_order[None, :] == jnp.arange(27, dtype=jnp.int32)[:, None]).astype(jnp.float32)
    picked = jnp.einsum('tq,qio->tio', chosen, stored.astype(jnp.float32), precision=lax.Precision.HIGHEST)
    return picked.astype(jnp.bfloat16)

def volume_conv(values, kernel):
    weights = jnp.transpose(kernel.astype(jnp.float32).reshape(3, 3, 3, kernel.shape[1], kernel.shape[2]), (4, 3, 0, 1, 2))
    return lax.conv_general_dilated(values[None], weights, (1, 1, 1), ((1, 1), (1, 1), (1, 1)), dimension_numbers=('NCDHW', 'OIDHW', 'NCDHW'), precision=lax.Precision.HIGHEST)[0]

def denoise(field, kernel_one, first_bias, kernel_two, second_bias):
    field_low = lax.optimization_barrier(field.astype(jnp.bfloat16)).astype(jnp.float32)
    groups = HID // 8
    one_groups = jnp.transpose(kernel_one.reshape(27, 2, groups, 8), (2, 0, 1, 3))
    two_groups = jnp.transpose(kernel_two.reshape(27, groups, 8, 2), (1, 0, 2, 3))
    bias_groups = first_bias.reshape(groups, 8)

    def group_step(running, inputs):
        one_part, bias_part, two_part = inputs
        hidden = jax.nn.relu(volume_conv(field_low, one_part) + bias_part[:, None, None, None]).astype(jnp.bfloat16)
        hidden = lax.optimization_barrier(hidden)
        return (running + volume_conv(hidden.astype(jnp.float32), two_part), None)
    summed = lax.scan(group_step, jnp.zeros_like(field), (one_groups, bias_groups, two_groups))[0]
    return summed + second_bias[:, None, None, None]

def reference(kspace, coil_maps, sample_mask, tap_order, first_kernel, first_bias, second_kernel, second_bias):
    tables = (make_table(W, -1.0), make_table(H, -1.0), make_table(S, -1.0), make_table(W, 1.0), make_table(H, 1.0), make_table(S, 1.0))
    measured = jnp.moveaxis(kspace.reshape(2, S, C, H, W), 2, 0)
    maps_by_coil = jnp.moveaxis(coil_maps, 2, 0)
    sampled_lines = jnp.moveaxis(sample_mask, 1, 0).astype(jnp.float32)[:, None, :, :, None]
    empty_sum = jnp.zeros((2, S, H, W), jnp.float32)

    def data_step(running, inputs):
        measured_coil, map_coil, line_coil = inputs
        residual = (line_coil * measured_coil.astype(jnp.float32)).astype(jnp.bfloat16)
        return (running + coil_adjoint(residual, map_coil, tables), None)
    estimate = lax.scan(data_step, empty_sum, (measured, maps_by_coil, sampled_lines))[0]

    def normal_op(image):

        def coil_step(running, inputs):
            measured_coil, map_coil, line_coil = inputs
            spectrum = coil_forward(image, map_coil, tables)
            residual = (line_coil * (spectrum - measured_coil.astype(jnp.float32))).astype(jnp.bfloat16)
            return (running + coil_adjoint(residual, map_coil, tables), None)
        return lax.scan(coil_step, empty_sum, (measured, maps_by_coil, sampled_lines))[0]
    kernel_one = tap_kernel(tap_order, first_kernel)
    kernel_two = tap_kernel(tap_order, second_kernel)
    dual_var = jnp.zeros_like(estimate)
    for iteration in range(ITERS):
        before = estimate - dual_var
        update = before - normal_op(before)
        denoiser_in = update + dual_var
        estimate = denoiser_in - denoise(denoiser_in, kernel_one, first_bias, kernel_two, second_bias)
        dual_var = dual_var + update - estimate
    return (estimate, dual_var)
```

```python
import math

import jax
import jax.numpy as jnp
from jax import lax
from jax.experimental import pallas as pl
from jax.experimental.pallas import tpu as pltpu
from jax.sharding import PartitionSpec as P

LOW = jnp.bfloat16
FULL = jnp.float32
VMEM = pl.BlockSpec(memory_space=pltpu.VMEM)
SMEM = pl.BlockSpec(memory_space=pltpu.SMEM)


def make_table(length, direction):
    positions = lax.optimization_barrier(jnp.arange(length, dtype=jnp.int32))
    product = positions[:, None] * positions[None, :] % length
    angles = 2.0 * math.pi / length * product.astype(FULL)
    norm_scale = 1.0 / math.sqrt(length)
    real_t = (jnp.cos(angles) * norm_scale).astype(LOW)
    imag_t = (direction * jnp.sin(angles) * norm_scale).astype(LOW)
    upper = jnp.stack([real_t, imag_t], axis=1)
    lower = jnp.stack([-imag_t, real_t], axis=1)
    return jnp.stack([upper, lower])


def spread_table(table, copies):
    size = table.shape[1]
    square = table.reshape(2 * size, 2 * size)
    wide = 2 * size * copies
    pick = (jnp.arange(wide)[:, None] // copies == jnp.arange(2 * size)[None, :]).astype(LOW)
    rows = einsum("ra,ba->rb", pick, square).astype(LOW)
    full = einsum("rb,cb->rc", rows, pick)
    same = jnp.arange(wide)[:, None] % copies == jnp.arange(wide)[None, :] % copies
    return jnp.where(same, full, 0.0).astype(LOW)


def tap_kernel(tap_order, stored):
    chosen = (tap_order[None, :] == jnp.arange(27, dtype=jnp.int32)[:, None]).astype(LOW)
    return einsum("tq,qio->tio", chosen, stored).astype(LOW)


def einsum(pattern, a, b):
    return jnp.einsum(pattern, a, b, preferred_element_type=FULL)


def swap(blocks):
    return lax.all_to_all(blocks, "slc", split_axis=0, concat_axis=0, tiled=True)


def matmul(a, b, dims=((1,), (0,))):
    return lax.dot_general(a, b, (dims, ((), ())), preferred_element_type=FULL)


def data_kernel(s_ref, u_ref, mask_ref, back_src, fwd, back, zf_ref, zb_ref, out_ref, ad_ref, sum_ref):
    n, coils, _, depth, cols, H = s_ref.shape
    slices = n * depth
    rows = slices * cols
    lines = u_ref.shape[2] // 2

    def sens(c):
        return [s_ref[:, c, p].astype(FULL).reshape(rows, H) for p in range(2)]

    ad_ref[...] = jnp.zeros_like(ad_ref)
    sum_ref[...] = jnp.zeros_like(sum_ref)

    def combine(total_ref, s, image):
        r, i = image[:, :H], image[:, H:]
        total_ref[0] += s[0] * r + s[1] * i
        total_ref[1] += s[0] * i - s[1] * r

    @pl.loop(0, coils)
    def _(c):
        u = u_ref[:, c].reshape(n * 2 * lines, rows)
        combine(ad_ref, sens(c), matmul(u, back_src[...], ((0,), (0,))))

    @pl.loop(0, coils // 2)
    def _(c2):
        pair = []
        for c in (2 * c2, 2 * c2 + 1):
            s = sens(c)
            v = [ad_ref[0], ad_ref[1]]
            w = jnp.concatenate([s[0] * v[0] - s[1] * v[1], s[0] * v[1] + s[1] * v[0]], axis=1)
            f = matmul(w.astype(LOW), fwd[...]).astype(LOW)
            pair.append(jnp.concatenate([f[:, :H], f[:, H:]], axis=0))
        g = matmul(zf_ref[...], jnp.concatenate(pair, axis=1))
        keep = []
        for k, c in enumerate((2 * c2, 2 * c2 + 1)):
            m = jnp.broadcast_to(mask_ref[c][:, None, :], (slices, cols, H)).reshape(rows, H)
            part = g[:, k * H : (k + 1) * H]
            keep.append(jnp.concatenate([part[:rows] * m, part[rows:] * m], axis=0))
        h = matmul(zb_ref[...], jnp.concatenate(keep, axis=1).astype(LOW)).astype(LOW)
        for k, c in enumerate((2 * c2, 2 * c2 + 1)):
            part = h[:, k * H : (k + 1) * H]
            t = matmul(jnp.concatenate([part[:rows], part[rows:]], axis=1), back[...])
            combine(sum_ref, sens(c), t)

    for q in range(2):
        update = 2.0 * ad_ref[q] - sum_ref[q]
        for d in range(n):
            for k in range(depth + 4):
                z = d * depth - 2 + k
                if 0 <= z < slices:
                    out_ref[d, q, k] = update[z * cols : (z + 1) * cols].astype(LOW)
                else:
                    out_ref[d, q, k] = jnp.zeros((cols, H), LOW)


def data_step(maps, spectra, mask, tables):
    n, coils, _, depth, cols, H = maps.shape
    rows = n * depth * cols
    return pl.pallas_call(
        data_kernel,
        out_shape=jax.ShapeDtypeStruct((n, 2, depth + 4, cols, H), LOW),
        in_specs=[VMEM] * (3 + len(tables)),
        out_specs=VMEM,
        scratch_shapes=[pltpu.VMEM((2, rows, H), FULL), pltpu.VMEM((2, rows, H), FULL)],
    )(maps, spectra, mask, *tables)


def data_step_plain(maps, spectra, mask, table_f, table_g, depth_f, depth_g):
    n, coils, _, depth, cols, H = maps.shape
    slices = n * depth
    sens = maps.astype(FULL).transpose(2, 1, 4, 0, 3, 5).reshape(2, coils, cols, slices, H)
    part = spectra.reshape(n, coils, 2, H // n, slices, cols)
    part = part.transpose(2, 1, 5, 4, 0, 3).reshape(2, coils, cols, slices, H)

    def combine(image):
        return jnp.stack([
            jnp.sum(sens[0] * image[0] + sens[1] * image[1], axis=0),
            jnp.sum(sens[0] * image[1] - sens[1] * image[0], axis=0),
        ])

    v = combine(einsum("pcxzj,pjqk->qcxzk", part, table_g))
    w = jnp.stack([sens[0] * v[0] - sens[1] * v[1], sens[0] * v[1] + sens[1] * v[0]]).astype(LOW)
    f = einsum("pcxzj,pjqk->qcxzk", w, table_f).astype(LOW)
    g = einsum("pcxjk,pjqz->qcxzk", f, depth_f) * mask[:, None]
    h = einsum("pcxjk,pjqz->qcxzk", g.astype(LOW), depth_g).astype(LOW)
    update = 2.0 * v - combine(einsum("pcxzj,pjqk->qcxzk", h, table_g))
    padded = jnp.pad(update.astype(LOW), ((0, 0), (0, 0), (2, 2), (0, 0)))
    sent = jnp.stack([padded[:, :, d * depth : d * depth + depth + 4] for d in range(n)])
    return sent.transpose(0, 1, 3, 2, 4)


GROUP = 8
STEP = 4


def denoise_kernel(base_ref, w_ref, one_ref, bias_ref, two_ref, last_ref, est_ref, dual_ref, cols, acc):
    blocks, _, window, _, L = w_ref.shape
    R = blocks * GROUP
    depth = window - 4
    slices = base_ref[1]
    lane = lax.broadcasted_iota(jnp.int32, (R, L), 1)
    row = lax.broadcasted_iota(jnp.int32, (R, L), 0)

    def field(i, z):
        return w_ref[:, i, z].astype(FULL).reshape(R, L)

    for z in range(window):
        for side in range(3):
            parts = ([], [])
            for i in range(2):
                f = field(i, z)
                if side == 0:
                    f = jnp.where(lane == 0, 0.0, pltpu.roll(f, 1, axis=1))
                if side == 2:
                    f = jnp.where(lane == L - 1, 0.0, pltpu.roll(f, L - 1, axis=1))
                down = jnp.where(row < 2, 0.0, pltpu.roll(f, 2, axis=0))
                up = jnp.where(row >= R - 2, 0.0, pltpu.roll(f, R - 2, axis=0))
                parts[0].append(down.reshape(blocks, GROUP, L))
                parts[1].append(up.reshape(blocks, GROUP, L))
            for phase in range(2):
                cols[phase, z, side] = jnp.concatenate(parts[phase], axis=1).astype(LOW)

    low_lane = lax.broadcasted_iota(jnp.int32, (1, 2 * L), 1) < L
    small_lane = lax.broadcasted_iota(jnp.int32, (2 * GROUP, L), 1)

    def live(k):
        z = base_ref[0] - 1 + k
        return jnp.where((z >= 0) & (z < slices), 1.0, 0.0)

    keep = [jnp.where(low_lane, live(2 * k), live(2 * k + 1)) for k in range(2)]

    @pl.loop(0, blocks)
    def _(j):
        for phase in range(2):

            def gathered(k):
                return jnp.concatenate(
                    [cols[phase, k + a, b, j] for a in range(3) for b in range(3)], axis=0
                )

            hidden = []
            for k in range(2):
                patch = jnp.concatenate([gathered(2 * k), gathered(2 * k + 1)], axis=1)
                summed = matmul(one_ref[...], patch) + bias_ref[...]
                hidden.append((jnp.maximum(summed, 0.0) * keep[k]).astype(LOW))
            middle = jnp.concatenate([hidden[0][:, L:], hidden[1][:, :L]], axis=1)
            terms = matmul(two_ref[...], jnp.concatenate([hidden[0], middle, hidden[1]], axis=0))
            width = 2 * GROUP
            for z in range(2):
                left, mid, right = [
                    terms[s * width : (s + 1) * width, z * L : (z + 1) * L] for s in range(3)
                ]
                left = jnp.where(small_lane == 0, 0.0, pltpu.roll(left, 1, axis=1))
                right = jnp.where(small_lane == L - 1, 0.0, pltpu.roll(right, L - 1, axis=1))
                both = left + mid + right
                for o in range(2):
                    acc[phase, z, o, j] = both[o * GROUP : (o + 1) * GROUP]

    for z in range(depth):
        for o in range(2):
            even = pltpu.roll(acc[0, z, o].reshape(R, L), R - 2, axis=0)
            odd = pltpu.roll(acc[1, z, o].reshape(R, L), 2, axis=0)
            noise = jnp.where(row >= R - 2, 0.0, even) + jnp.where(row < 2, 0.0, odd) + last_ref[o]
            est_ref[o, z] = jnp.transpose(field(o, z + 2) - noise)
            dual_ref[o, z] = jnp.transpose(noise)


def denoise(base, window, one, bias, two, last):
    blocks, _, spread, group, L = window.shape
    depth = spread - 4
    R = blocks * group
    taps_one = one.reshape(3, 3, 3, 2, -1)
    taps_two = two.reshape(3, 3, 3, -1, 2)
    hid = taps_one.shape[-1]
    dx, rr, rb = jnp.arange(3), jnp.arange(GROUP), jnp.arange(STEP)
    into = (dx[:, None, None] == rr[None, :, None] - rb[None, None, :] - 1).astype(LOW)
    out = (dx[:, None, None] == rb[None, None, :] - rr[None, :, None] + 3).astype(LOW)
    first = einsum("abxio,xrk->koabir", taps_one, into).astype(LOW).reshape(STEP * hid, 18 * GROUP)
    second = einsum("abxoc,xrk->bcrako", taps_two, out).astype(LOW).reshape(6 * GROUP, 3 * STEP * hid)
    bias = jnp.tile(bias, STEP)[:, None]
    shape = jax.ShapeDtypeStruct((2, depth, L, R), FULL)
    return pl.pallas_call(
        denoise_kernel,
        out_shape=(shape, shape),
        in_specs=[SMEM, VMEM, VMEM, VMEM, VMEM, SMEM],
        out_specs=(VMEM, VMEM),
        scratch_shapes=[
            pltpu.VMEM((2, spread, 3, blocks, 2 * GROUP, L), LOW),
            pltpu.VMEM((2, depth, 2, blocks, GROUP, L), FULL),
        ],
    )(base, window, first, bias, second, last)


def on_device(
    kspace, coil_maps, sample_mask, tap_order, first_kernel, first_bias, second_kernel, second_bias
):
    n = lax.axis_size("slc")
    position = lax.axis_index("slc")
    _, depth, coils, H, W = coil_maps.shape
    slices, points = kspace.shape[1], kspace.shape[3]
    lines = points // W
    ncol = W // n

    maps = coil_maps.reshape(2, depth, coils, H, n, ncol).transpose(4, 2, 0, 1, 5, 3)
    maps = swap(maps)

    table_f, table_g = make_table(H, -1.0), make_table(H, 1.0)
    depth_f, depth_g = make_table(slices, -1.0), make_table(slices, 1.0)
    own_mask = lax.dynamic_slice_in_dim(sample_mask, position * lines, lines, axis=2)
    masked = kspace.reshape(2, slices, coils, lines, W) * own_mask.astype(LOW)[None, ..., None]
    by_x = einsum("pzcrj,pjqk->qzcrk", masked, make_table(W, 1.0)).astype(LOW)
    by_z = einsum("pjcrx,pjqk->xcqrk", by_x, depth_g).astype(LOW)
    by_z = by_z.reshape(n, ncol, coils, 2 * lines, slices).transpose(0, 2, 3, 4, 1)
    by_z = by_z.reshape(n, coils, 2 * lines, slices * ncol)
    by_z, maps = lax.optimization_barrier((by_z, maps))
    spectra = swap(by_z)

    mask = sample_mask.astype(FULL).transpose(1, 0, 2)
    if ncol == GROUP:
        back_src = table_g.reshape(2, n, lines, 2 * H).transpose(1, 0, 2, 3).reshape(2 * H, 2 * H)
        tables = (
            back_src,
            table_f.reshape(2 * H, 2 * H),
            table_g.reshape(2 * H, 2 * H),
            spread_table(depth_f, ncol),
            spread_table(depth_g, ncol),
        )
        sent = data_step(maps, spectra, mask, tables)
    else:
        sent = data_step_plain(maps, spectra, mask, table_f, table_g, depth_f, depth_g)
    got = swap(sent)
    if ncol != GROUP:
        got = got.transpose(0, 3, 1, 2, 4).reshape(W // GROUP, GROUP, 2, depth + 4, H)
        got = got.transpose(0, 2, 3, 1, 4)

    kernel_one = tap_kernel(tap_order, first_kernel)
    kernel_two = tap_kernel(tap_order, second_kernel)
    base = jnp.stack([position * depth, jnp.int32(slices)]).astype(jnp.int32)
    return denoise(base, got, kernel_one, first_bias, kernel_two, second_bias)


def solution(mesh):
    placed = (
        P("grp", None, None, "slc"),
        P("grp", "slc", None, None, None),
        P("grp", None, None),
        P(),
        P(),
        P(),
        P(),
        P(),
    )
    return jax.shard_map(
        on_device,
        mesh=mesh,
        in_specs=placed,
        out_specs=(P("grp", "slc", None, None), P("grp", "slc", None, None)),
        check_vma=False,
    )
```

```python
import math

import jax
import jax.numpy as jnp
from jax import lax
from jax.experimental import pallas as pl
from jax.experimental.pallas import tpu as pltpu
from jax.sharding import PartitionSpec as P

LOW = jnp.bfloat16
FULL = jnp.float32
VMEM = pl.BlockSpec(memory_space=pltpu.VMEM)
SMEM = pl.BlockSpec(memory_space=pltpu.SMEM)


def make_table(length, direction):
    positions = lax.optimization_barrier(jnp.arange(length, dtype=jnp.int32))
    product = positions[:, None] * positions[None, :] % length
    angles = 2.0 * math.pi / length * product.astype(FULL)
    norm_scale = 1.0 / math.sqrt(length)
    real_t = (jnp.cos(angles) * norm_scale).astype(LOW)
    imag_t = (direction * jnp.sin(angles) * norm_scale).astype(LOW)
    upper = jnp.stack([real_t, imag_t], axis=1)
    lower = jnp.stack([-imag_t, real_t], axis=1)
    return jnp.stack([upper, lower])


def spread_table(table, copies):
    size = table.shape[1]
    square = table.reshape(2 * size, 2 * size)
    wide = 2 * size * copies
    pick = (jnp.arange(wide)[:, None] // copies == jnp.arange(2 * size)[None, :]).astype(LOW)
    rows = einsum("ra,ba->rb", pick, square).astype(LOW)
    full = einsum("rb,cb->rc", rows, pick)
    same = jnp.arange(wide)[:, None] % copies == jnp.arange(wide)[None, :] % copies
    return jnp.where(same, full, 0.0).astype(LOW)


def tap_kernel(tap_order, stored):
    chosen = (tap_order[None, :] == jnp.arange(27, dtype=jnp.int32)[:, None]).astype(LOW)
    return einsum("tq,qio->tio", chosen, stored).astype(LOW)


def einsum(pattern, a, b):
    return jnp.einsum(pattern, a, b, preferred_element_type=FULL)


def swap(blocks):
    return lax.all_to_all(blocks, "slc", split_axis=0, concat_axis=0, tiled=True)


def matmul(a, b, dims=((1,), (0,))):
    return lax.dot_general(a, b, (dims, ((), ())), preferred_element_type=FULL)


def point_kernel(place_ref, k_ref, mask_ref, table_ref, depth_ref, out_ref, by_x, turned):
    _, slices, coils, _ = k_ref.shape
    n, _, twice, _ = out_ref.shape
    lines = twice // 2
    W = table_ref.shape[0] // 2
    cols = W // n

    @pl.loop(0, slices)
    def _(z):
        rows = jnp.concatenate(
            [
                jnp.concatenate([k_ref[p, z, :, r * W : (r + 1) * W] for p in range(2)], axis=1)
                for r in range(lines)
            ],
            axis=0,
        )
        image = matmul(table_ref[...], rows, ((1,), (1,))) * mask_ref[pl.ds(z, 1), :]
        for p in range(2):
            by_x[:, p, z] = image[p * W : (p + 1) * W].reshape(n, cols, lines * coils)

    @pl.loop(0, n)
    def _(k):
        own = by_x[lax.rem(place_ref[0] + k, n)].reshape(2 * slices * cols, lines * coils).astype(LOW)
        full = matmul(own, depth_ref[...], ((0,), (0,)))
        tiles, _, lane = turned.shape
        for t in range(tiles):
            turned[t] = full[:, t * lane : (t + 1) * lane]
        for c in range(coils):
            picked = [turned[t, pl.ds(c, lines, stride=coils), :] for t in range(tiles)]
            both = [jnp.concatenate(picked[q * tiles // 2 : (q + 1) * tiles // 2], axis=1) for q in range(2)]
            out_ref[k, c] = jnp.concatenate(both, axis=0).astype(LOW)


def point_step(place, kspace, mask, table, depth_table, n):
    _, slices, coils, points = kspace.shape
    W = table.shape[0] // 2
    lines, cols = points // W, W // n
    return pl.pallas_call(
        point_kernel,
        out_shape=jax.ShapeDtypeStruct((n, coils, 2 * lines, slices * cols), LOW),
        in_specs=[SMEM] + [VMEM] * 4,
        out_specs=VMEM,
        scratch_shapes=[
            pltpu.VMEM((n, 2, slices, cols, lines * coils), FULL),
            pltpu.VMEM((2 * slices * cols // W, lines * coils, W), FULL),
        ],
    )(place, kspace, mask, table, depth_table)


def data_kernel(place_ref, s_ref, mask_ref, back_src, fwd, back, zf_ref, zb_ref, *refs):
    n, coils, _, depth, cols, H = s_ref.shape
    received, (out_ref, u_ref, ad_ref, sum_ref) = refs[:n], refs[n:]
    slices = n * depth
    rows = slices * cols
    lines = u_ref.shape[2] // 2
    for k in range(n):
        u_ref[lax.rem(place_ref[0] + n - k, n)] = received[k][...]

    def sens(c):
        return [s_ref[:, c, p].astype(FULL).reshape(rows, H) for p in range(2)]

    ad_ref[...] = jnp.zeros_like(ad_ref)
    sum_ref[...] = jnp.zeros_like(sum_ref)

    def combine(total_ref, s, image):
        r, i = image[:, :H], image[:, H:]
        total_ref[0] += s[0] * r + s[1] * i
        total_ref[1] += s[0] * i - s[1] * r

    @pl.loop(0, coils)
    def _(c):
        u = u_ref[:, c].reshape(n * 2 * lines, rows)
        combine(ad_ref, sens(c), matmul(u, back_src[...], ((0,), (0,))))

    @pl.loop(0, coils // 2)
    def _(c2):
        pair = []
        for c in (2 * c2, 2 * c2 + 1):
            s = sens(c)
            v = [ad_ref[0], ad_ref[1]]
            w = jnp.concatenate([s[0] * v[0] - s[1] * v[1], s[0] * v[1] + s[1] * v[0]], axis=1)
            f = matmul(w.astype(LOW), fwd[...]).astype(LOW)
            pair.append(jnp.concatenate([f[:, :H], f[:, H:]], axis=0))
        g = matmul(zf_ref[...], jnp.concatenate(pair, axis=1))
        keep = []
        for k, c in enumerate((2 * c2, 2 * c2 + 1)):
            m = jnp.broadcast_to(mask_ref[c][:, None, :], (slices, cols, H)).reshape(rows, H)
            part = g[:, k * H : (k + 1) * H]
            keep.append(jnp.concatenate([part[:rows] * m, part[rows:] * m], axis=0))
        h = matmul(zb_ref[...], jnp.concatenate(keep, axis=1).astype(LOW)).astype(LOW)
        for k, c in enumerate((2 * c2, 2 * c2 + 1)):
            part = h[:, k * H : (k + 1) * H]
            t = matmul(jnp.concatenate([part[:rows], part[rows:]], axis=1), back[...])
            combine(sum_ref, sens(c), t)

    for q in range(2):
        update = 2.0 * ad_ref[q] - sum_ref[q]
        for d in range(n):
            for k in range(depth + 4):
                z = d * depth - 2 + k
                if 0 <= z < slices:
                    out_ref[d, q, k] = update[z * cols : (z + 1) * cols].astype(LOW)
                else:
                    out_ref[d, q, k] = jnp.zeros((cols, H), LOW)


def data_step(place, maps, blocks, mask, tables):
    n, coils, _, depth, cols, H = maps.shape
    rows = n * depth * cols
    return pl.pallas_call(
        data_kernel,
        out_shape=jax.ShapeDtypeStruct((n, 2, depth + 4, cols, H), LOW),
        in_specs=[SMEM] + [VMEM] * (2 + len(tables) + n),
        out_specs=VMEM,
        scratch_shapes=[
            pltpu.VMEM((n, *blocks[0].shape), LOW),
            pltpu.VMEM((2, rows, H), FULL),
            pltpu.VMEM((2, rows, H), FULL),
        ],
    )(place, maps, mask, *tables, *blocks)


def data_step_plain(maps, spectra, mask, table_f, table_g, depth_f, depth_g):
    n, coils, _, depth, cols, H = maps.shape
    slices = n * depth
    sens = maps.astype(FULL).transpose(2, 1, 4, 0, 3, 5).reshape(2, coils, cols, slices, H)
    part = spectra.reshape(n, coils, 2, H // n, slices, cols)
    part = part.transpose(2, 1, 5, 4, 0, 3).reshape(2, coils, cols, slices, H)

    def combine(image):
        return jnp.stack([
            jnp.sum(sens[0] * image[0] + sens[1] * image[1], axis=0),
            jnp.sum(sens[0] * image[1] - sens[1] * image[0], axis=0),
        ])

    v = combine(einsum("pcxzj,pjqk->qcxzk", part, table_g))
    w = jnp.stack([sens[0] * v[0] - sens[1] * v[1], sens[0] * v[1] + sens[1] * v[0]]).astype(LOW)
    f = einsum("pcxzj,pjqk->qcxzk", w, table_f).astype(LOW)
    g = einsum("pcxjk,pjqz->qcxzk", f, depth_f) * mask[:, None]
    h = einsum("pcxjk,pjqz->qcxzk", g.astype(LOW), depth_g).astype(LOW)
    update = 2.0 * v - combine(einsum("pcxzj,pjqk->qcxzk", h, table_g))
    padded = jnp.pad(update.astype(LOW), ((0, 0), (0, 0), (2, 2), (0, 0)))
    sent = jnp.stack([padded[:, :, d * depth : d * depth + depth + 4] for d in range(n)])
    return sent.transpose(0, 1, 3, 2, 4)


GROUP = 8
STEP = 4


def denoise_kernel(base_ref, w_ref, one_ref, bias_ref, two_ref, last_ref, est_ref, dual_ref, cols, acc):
    blocks, _, window, _, L = w_ref.shape
    R = blocks * GROUP
    depth = window - 4
    slices = base_ref[1]
    lane = lax.broadcasted_iota(jnp.int32, (R, L), 1)
    row = lax.broadcasted_iota(jnp.int32, (R, L), 0)

    def field(i, z):
        return w_ref[:, i, z].astype(FULL).reshape(R, L)

    for z in range(window):
        for side in range(3):
            parts = ([], [])
            for i in range(2):
                f = field(i, z)
                if side == 0:
                    f = jnp.where(lane == 0, 0.0, pltpu.roll(f, 1, axis=1))
                if side == 2:
                    f = jnp.where(lane == L - 1, 0.0, pltpu.roll(f, L - 1, axis=1))
                down = jnp.where(row < 2, 0.0, pltpu.roll(f, 2, axis=0))
                up = jnp.where(row >= R - 2, 0.0, pltpu.roll(f, R - 2, axis=0))
                parts[0].append(down.reshape(blocks, GROUP, L))
                parts[1].append(up.reshape(blocks, GROUP, L))
            for phase in range(2):
                cols[phase, z, side] = jnp.concatenate(parts[phase], axis=1).astype(LOW)

    low_lane = lax.broadcasted_iota(jnp.int32, (1, 2 * L), 1) < L
    small_lane = lax.broadcasted_iota(jnp.int32, (2 * GROUP, L), 1)

    def live(k):
        z = base_ref[0] - 1 + k
        return jnp.where((z >= 0) & (z < slices), 1.0, 0.0)

    keep = [jnp.where(low_lane, live(2 * k), live(2 * k + 1)) for k in range(2)]

    @pl.loop(0, blocks)
    def _(j):
        for phase in range(2):

            def gathered(k):
                return jnp.concatenate(
                    [cols[phase, k + a, b, j] for a in range(3) for b in range(3)], axis=0
                )

            hidden = []
            for k in range(2):
                patch = jnp.concatenate([gathered(2 * k), gathered(2 * k + 1)], axis=1)
                summed = matmul(one_ref[...], patch) + bias_ref[...]
                hidden.append((jnp.maximum(summed, 0.0) * keep[k]).astype(LOW))
            middle = jnp.concatenate([hidden[0][:, L:], hidden[1][:, :L]], axis=1)
            terms = matmul(two_ref[...], jnp.concatenate([hidden[0], middle, hidden[1]], axis=0))
            width = 2 * GROUP
            for z in range(2):
                left, mid, right = [
                    terms[s * width : (s + 1) * width, z * L : (z + 1) * L] for s in range(3)
                ]
                left = jnp.where(small_lane == 0, 0.0, pltpu.roll(left, 1, axis=1))
                right = jnp.where(small_lane == L - 1, 0.0, pltpu.roll(right, L - 1, axis=1))
                both = left + mid + right
                for o in range(2):
                    acc[phase, z, o, j] = both[o * GROUP : (o + 1) * GROUP]

    for z in range(depth):
        for o in range(2):
            even = pltpu.roll(acc[0, z, o].reshape(R, L), R - 2, axis=0)
            odd = pltpu.roll(acc[1, z, o].reshape(R, L), 2, axis=0)
            noise = jnp.where(row >= R - 2, 0.0, even) + jnp.where(row < 2, 0.0, odd) + last_ref[o]
            est_ref[o, z] = jnp.transpose(field(o, z + 2) - noise)
            dual_ref[o, z] = jnp.transpose(noise)


def denoise(base, window, one, bias, two, last):
    blocks, _, spread, group, L = window.shape
    depth = spread - 4
    R = blocks * group
    taps_one = one.reshape(3, 3, 3, 2, -1)
    taps_two = two.reshape(3, 3, 3, -1, 2)
    hid = taps_one.shape[-1]
    dx, rr, rb = jnp.arange(3), jnp.arange(GROUP), jnp.arange(STEP)
    into = (dx[:, None, None] == rr[None, :, None] - rb[None, None, :] - 1).astype(LOW)
    out = (dx[:, None, None] == rb[None, None, :] - rr[None, :, None] + 3).astype(LOW)
    first = einsum("abxio,xrk->koabir", taps_one, into).astype(LOW).reshape(STEP * hid, 18 * GROUP)
    second = einsum("abxoc,xrk->bcrako", taps_two, out).astype(LOW).reshape(6 * GROUP, 3 * STEP * hid)
    bias = jnp.tile(bias, STEP)[:, None]
    shape = jax.ShapeDtypeStruct((2, depth, L, R), FULL)
    return pl.pallas_call(
        denoise_kernel,
        out_shape=(shape, shape),
        in_specs=[SMEM, VMEM, VMEM, VMEM, VMEM, SMEM],
        out_specs=(VMEM, VMEM),
        scratch_shapes=[
            pltpu.VMEM((2, spread, 3, blocks, 2 * GROUP, L), LOW),
            pltpu.VMEM((2, depth, 2, blocks, GROUP, L), FULL),
        ],
    )(base, window, first, bias, second, last)


def on_device(
    kspace, coil_maps, sample_mask, tap_order, first_kernel, first_bias, second_kernel, second_bias
):
    n = lax.axis_size("slc")
    position = lax.axis_index("slc")
    _, depth, coils, H, W = coil_maps.shape
    slices, points = kspace.shape[1], kspace.shape[3]
    lines = points // W
    ncol = W // n

    maps = coil_maps.reshape(2, depth, coils, H, n, ncol).transpose(4, 2, 0, 1, 5, 3)
    maps = swap(maps)

    table_f, table_g = make_table(H, -1.0), make_table(H, 1.0)
    depth_f, depth_g = make_table(slices, -1.0), make_table(slices, 1.0)
    place = position.astype(jnp.int32)[None]
    own_mask = lax.dynamic_slice_in_dim(sample_mask, position * lines, lines, axis=2)
    fits = ncol == GROUP and coils * lines == W
    if fits:
        own_mask = own_mask.transpose(0, 2, 1).reshape(slices, lines * coils).astype(FULL)
        table_x = make_table(W, 1.0).reshape(2 * W, 2 * W)
        by_z = point_step(place, kspace, own_mask, table_x.T, spread_table(depth_g, ncol).T, n)
        blocks = [by_z[0]] + [
            lax.ppermute(by_z[k], "slc", [(i, (i + k) % n) for i in range(n)]) for k in range(1, n)
        ]
    else:
        masked = kspace.reshape(2, slices, coils, lines, W) * own_mask.astype(LOW)[None, ..., None]
        by_x = einsum("pzcrj,pjqk->qzcrk", masked, make_table(W, 1.0)).astype(LOW)
        by_z = einsum("pjcrx,pjqk->xcqrk", by_x, depth_g).astype(LOW)
        by_z = by_z.reshape(n, ncol, coils, 2 * lines, slices).transpose(0, 2, 3, 4, 1)
        spectra = swap(by_z.reshape(n, coils, 2 * lines, slices * ncol))

    mask = sample_mask.astype(FULL).transpose(1, 0, 2)
    if fits:
        back_src = table_g.reshape(2, n, lines, 2 * H).transpose(1, 0, 2, 3).reshape(2 * H, 2 * H)
        tables = (
            back_src,
            table_f.reshape(2 * H, 2 * H),
            table_g.reshape(2 * H, 2 * H),
            spread_table(depth_f, ncol),
            spread_table(depth_g, ncol),
        )
        sent = data_step(place, maps, blocks, mask, tables)
    else:
        sent = data_step_plain(maps, spectra, mask, table_f, table_g, depth_f, depth_g)
    got = swap(sent)
    if ncol != GROUP:
        got = got.transpose(0, 3, 1, 2, 4).reshape(W // GROUP, GROUP, 2, depth + 4, H)
        got = got.transpose(0, 2, 3, 1, 4)

    kernel_one = tap_kernel(tap_order, first_kernel)
    kernel_two = tap_kernel(tap_order, second_kernel)
    base = jnp.stack([position * depth, jnp.int32(slices)]).astype(jnp.int32)
    return denoise(base, got, kernel_one, first_bias, kernel_two, second_bias)


def solution(mesh):
    placed = (
        P("grp", None, None, "slc"),
        P("grp", "slc", None, None, None),
        P("grp", None, None),
        P(),
        P(),
        P(),
        P(),
        P(),
    )
    return jax.shard_map(
        on_device,
        mesh=mesh,
        in_specs=placed,
        out_specs=(P("grp", "slc", None, None), P("grp", "slc", None, None)),
        check_vma=False,
    )
```

```python
import functools
import math

import jax
import jax.numpy as jnp
import numpy as np
from jax import lax
from jax.experimental import pallas as pl
from jax.experimental.pallas import tpu as pltpu
from jax.sharding import PartitionSpec as P

GROUP = 8
STEP = 4
SETS = 2
AT_ONCE = 16
MAPS_AT_ONCE = 4
LOW = jnp.bfloat16
FULL = jnp.float32
VMEM = pl.BlockSpec(memory_space=pltpu.VMEM)
SMEM = pl.BlockSpec(memory_space=pltpu.SMEM)


def make_table(length, direction):
    positions = np.arange(length)
    angles = 2.0 * math.pi / length * (positions[:, None] * positions[None, :] % length)
    real_t = np.cos(angles) / math.sqrt(length)
    imag_t = direction * np.sin(angles) / math.sqrt(length)
    upper = np.stack([real_t, imag_t], axis=1)
    lower = np.stack([-imag_t, real_t], axis=1)
    return np.stack([upper, lower]).astype(np.float32)


def spread_table(table, copies):
    size = 2 * table.shape[1]
    return np.kron(table.reshape(size, size).T, np.eye(copies, dtype=np.float32))


def low(table):
    return jnp.asarray(table, LOW)


def tap_kernel(tap_order, stored):
    chosen = (tap_order[None, :] == jnp.arange(27, dtype=jnp.int32)[:, None]).astype(LOW)
    return einsum("tq,qio->tio", chosen, stored).astype(LOW)


def einsum(pattern, a, b):
    return jnp.einsum(pattern, a, b, preferred_element_type=FULL)


def swap(blocks):
    return lax.all_to_all(blocks, "slc", split_axis=0, concat_axis=0, tiled=True)


def matmul(a, b, dims=((1,), (0,))):
    return lax.dot_general(a, b, (dims, ((), ())), preferred_element_type=FULL)


def maps_kernel(place_ref, m_ref, *refs):
    _, depth, coils, H, W = m_ref.shape
    outs, scratch = refs[:-1], refs[-1]
    n = len(outs)
    part = W // (n * SETS)
    for c in range(coils):
        for p in range(2):
            turned = [
                jnp.transpose(m_ref[p, z, c]).astype(FULL).reshape(n, SETS * part, H) for z in range(depth)
            ]
            for i in range(SETS):
                rows = [t[:, i * part : (i + 1) * part] for t in turned]
                scratch[:, i, c, p] = jnp.concatenate(rows, axis=1).astype(LOW)
    for k in range(n):
        outs[k][...] = scratch[lax.rem(place_ref[0] + k, n)]


def maps_step(place, coil_maps, n):
    _, depth, coils, H, W = coil_maps.shape
    rows = depth * W // (n * SETS)
    return pl.pallas_call(
        maps_kernel,
        grid=(coils // MAPS_AT_ONCE,),
        out_shape=[jax.ShapeDtypeStruct((SETS, coils, 2, rows, H), LOW)] * n,
        in_specs=[SMEM, pl.BlockSpec((2, depth, MAPS_AT_ONCE, H, W), lambda i: (0, 0, i, 0, 0))],
        out_specs=[pl.BlockSpec((SETS, MAPS_AT_ONCE, 2, rows, H), lambda i: (0, i, 0, 0, 0))] * n,
        scratch_shapes=[pltpu.VMEM((n, SETS, MAPS_AT_ONCE, 2, rows, H), LOW)],
    )(place, coil_maps)


def point_kernel(place_ref, k_ref, mask_ref, table_ref, depth_ref, *refs):
    _, slices, coils, _ = k_ref.shape
    whole, by_x, turned = refs[0], refs[-2], refs[-1]
    n, _, twice, _ = whole.shape
    lines = twice // 2
    W = table_ref.shape[0] // 2
    cols = W // n

    @pl.loop(0, slices)
    def _(z):
        rows = jnp.concatenate(
            [
                jnp.concatenate([k_ref[p, z, :, r * W : (r + 1) * W] for p in range(2)], axis=1)
                for r in range(lines)
            ],
            axis=0,
        )
        image = matmul(table_ref[...], rows, ((1,), (1,))) * mask_ref[pl.ds(z, 1), :]
        for p in range(2):
            by_x[:, p, z] = image[p * W : (p + 1) * W].reshape(n, cols, lines * coils)

    tiles, lane = turned.shape[1], turned.shape[3]
    each = tiles // SETS
    for k in range(n):
        d = lax.rem(place_ref[0] + k, n)
        own = by_x[d].reshape(2 * slices * cols, lines * coils).astype(LOW)
        full = matmul(own, depth_ref[...], ((0,), (0,)))
        for t in range(tiles):
            turned[k % 2, t] = full[:, t * lane : (t + 1) * lane]
        for c in range(coils):
            picked = [turned[k % 2, t, pl.ds(c, lines, stride=coils), :] for t in range(tiles)]
            for i in range(SETS):
                both = [
                    jnp.concatenate(picked[i * each + q * each // 2 :][: each // 2], axis=1)
                    for q in range(2)
                ]
                block = jnp.concatenate(both, axis=0).astype(LOW)
                if i == 0:
                    whole[d, c] = block
                else:
                    refs[1 + (i - 1) * n + k][c] = block


def point_step(place, kspace, mask, table, depth_table, n):
    _, slices, coils, points = kspace.shape
    W = table.shape[0] // 2
    lines, cols = points // W, W // n
    block = (coils, 2 * lines, slices * cols // SETS)
    return pl.pallas_call(
        point_kernel,
        out_shape=[jax.ShapeDtypeStruct((n, *block), LOW)] + [jax.ShapeDtypeStruct(block, LOW)] * (n * (SETS - 1)),
        in_specs=[SMEM] + [VMEM] * 4,
        out_specs=[VMEM] * (1 + n * (SETS - 1)),
        scratch_shapes=[
            pltpu.VMEM((n, 2, slices, cols, lines * coils), FULL),
            pltpu.VMEM((2, 2 * slices * cols // W, lines * coils, W), FULL),
        ],
    )(place, kspace, mask, table, depth_table)


def data_kernel(turn, n, place_ref, mask_ref, back_src, fwd, back, zf_ref, zb_ref, *refs):
    (out_ref, s_ref, ad_ref, sum_ref), sent = refs[-4:], refs[:-4]
    if len(sent) > n + 1:
        sent, u_ref = sent[:-1], sent[-1]
    _, coils, _, depth_cols, H = s_ref.shape
    rows = n * depth_cols
    for k in range(n):
        source = lax.rem(place_ref[0] + n - k, n)
        s_ref[source] = sent[k][turn]
        if len(sent) == 2 * n:
            u_ref[source] = sent[n + k][...]
    if len(sent) == n + 1:
        u_ref = sent[n]
    lines = u_ref.shape[2] // 2

    def sens(c):
        return [s_ref[:, c, p].astype(FULL).reshape(rows, H) for p in range(2)]

    def combine(total_ref, first, image):
        real, imag = total_ref[0], total_ref[1]
        for k in range(AT_ONCE):
            s = sens(first + k)
            r, i = image[k * rows : (k + 1) * rows, :H], image[k * rows : (k + 1) * rows, H:]
            real += s[0] * r + s[1] * i
            imag += s[0] * i - s[1] * r
        total_ref[0], total_ref[1] = real, imag

    ad_ref[...] = jnp.zeros_like(ad_ref)
    sum_ref[...] = jnp.zeros_like(sum_ref)

    @pl.loop(0, coils // AT_ONCE)
    def _(g):
        first = g * AT_ONCE
        u = [u_ref[:, first + k].reshape(n * 2 * lines, rows) for k in range(AT_ONCE)]
        combine(ad_ref, first, matmul(jnp.concatenate(u, axis=1), back_src[...], ((0,), (0,))))

    @pl.loop(0, coils // AT_ONCE)
    def _(g):
        first = g * AT_ONCE
        v = [ad_ref[0], ad_ref[1]]
        many = []
        for k in range(AT_ONCE):
            s = sens(first + k)
            both = [s[0] * v[0] - s[1] * v[1], s[0] * v[1] + s[1] * v[0]]
            many.append(jnp.concatenate(both, axis=1).astype(LOW))
        f = matmul(jnp.concatenate(many, axis=0), fwd[...]).astype(LOW)
        wide = []
        for k in range(AT_ONCE):
            part = f[k * rows : (k + 1) * rows]
            wide.append(jnp.concatenate([part[:, :H], part[:, H:]], axis=0))
        freq = matmul(zf_ref[...], jnp.concatenate(wide, axis=1))
        keep = []
        for k in range(AT_ONCE):
            part = freq[:, k * H : (k + 1) * H]
            m = mask_ref[first + k]
            keep.append(jnp.concatenate([part[:rows] * m, part[rows:] * m], axis=0))
        h = matmul(zb_ref[...], jnp.concatenate(keep, axis=1).astype(LOW)).astype(LOW)
        many = []
        for k in range(AT_ONCE):
            part = h[:, k * H : (k + 1) * H]
            many.append(jnp.concatenate([part[:rows], part[rows:]], axis=1))
        combine(sum_ref, first, matmul(jnp.concatenate(many, axis=0), back[...]))

    tall = out_ref.shape[2]
    edge = (tall - depth_cols) // 2
    for q in range(2):
        blank = jnp.zeros((edge, H), FULL)
        update = jnp.concatenate([blank, 2.0 * ad_ref[q] - sum_ref[q], blank], axis=0)
        for d in range(n):
            out_ref[d, q] = update[d * depth_cols : d * depth_cols + tall].astype(LOW)


def data_step(turn, n, place, maps, spectra, mask, tables):
    _, coils, _, depth_cols, H = maps[0].shape
    rows = n * depth_cols
    halo = 4 * (GROUP // SETS)
    scratch = [
        pltpu.VMEM((n, coils, 2, depth_cols, H), LOW),
        pltpu.VMEM((2, rows, H), FULL),
        pltpu.VMEM((2, rows, H), FULL),
    ]
    if len(spectra) == n:
        kernel = functools.partial(data_kernel_blocks, turn, n)
        scratch = scratch + [pltpu.VMEM((n, *spectra[0].shape), LOW)]
    else:
        kernel = functools.partial(data_kernel, turn, n)
    return pl.pallas_call(
        kernel,
        out_shape=jax.ShapeDtypeStruct((n, 2, depth_cols + halo, H), LOW),
        in_specs=[SMEM] + [VMEM] * (1 + len(tables) + n + len(spectra)),
        out_specs=VMEM,
        scratch_shapes=scratch,
    )(place, mask, *tables, *maps, *spectra)


def data_kernel_blocks(turn, n, *refs):
    data_kernel(turn, n, *refs[:-5], refs[-1], *refs[-5:-1])


def data_step_plain(maps, spectra, mask, table_f, table_g, depth_f, depth_g):
    n, coils, _, depth, cols, H = maps.shape
    slices = n * depth
    sens = maps.astype(FULL).transpose(2, 1, 4, 0, 3, 5).reshape(2, coils, cols, slices, H)
    part = spectra.reshape(n, coils, 2, H // n, slices, cols)
    part = part.transpose(2, 1, 5, 4, 0, 3).reshape(2, coils, cols, slices, H)

    def combine(image):
        return jnp.stack([
            jnp.sum(sens[0] * image[0] + sens[1] * image[1], axis=0),
            jnp.sum(sens[0] * image[1] - sens[1] * image[0], axis=0),
        ])

    v = combine(einsum("pcxzj,pjqk->qcxzk", part, table_g))
    w = jnp.stack([sens[0] * v[0] - sens[1] * v[1], sens[0] * v[1] + sens[1] * v[0]]).astype(LOW)
    f = einsum("pcxzj,pjqk->qcxzk", w, table_f).astype(LOW)
    g = einsum("pcxjk,pjqz->qcxzk", f, depth_f) * mask[:, None]
    h = einsum("pcxjk,pjqz->qcxzk", g.astype(LOW), depth_g).astype(LOW)
    update = 2.0 * v - combine(einsum("pcxzj,pjqk->qcxzk", h, table_g))
    padded = jnp.pad(update.astype(LOW), ((0, 0), (0, 0), (2, 2), (0, 0)))
    sent = jnp.stack([padded[:, :, d * depth : d * depth + depth + 4] for d in range(n)])
    return sent.transpose(0, 1, 3, 2, 4)


def denoise_kernel(base_ref, wa_ref, wb_ref, one_ref, two_ref, last_ref, est_ref, dual_ref, cols, acc):
    blocks, _, tall, L = wa_ref.shape
    part = GROUP // SETS
    window = tall // part
    R = blocks * GROUP
    depth = window - 4
    slices = base_ref[1]
    lane = lax.broadcasted_iota(jnp.int32, (R, L), 1)
    row = lax.broadcasted_iota(jnp.int32, (R, L), 0)

    def field(i, z):
        both = [
            ref[:, i].astype(FULL)[:, z * part : (z + 1) * part] for ref in (wa_ref, wb_ref)
        ]
        return jnp.concatenate(both, axis=1).reshape(R, L)

    for z in range(window):
        moved = ([], [])
        for i in range(2):
            f = field(i, z)
            moved[0].append(jnp.where(row < 2, 0.0, pltpu.roll(f, 2, axis=0)))
            moved[1].append(jnp.where(row >= R - 2, 0.0, pltpu.roll(f, R - 2, axis=0)))
        for phase in range(2):
            for side in range(3):
                parts = []
                for f in moved[phase]:
                    if side == 0:
                        f = jnp.where(lane == 0, 0.0, pltpu.roll(f, 1, axis=1))
                    if side == 2:
                        f = jnp.where(lane == L - 1, 0.0, pltpu.roll(f, L - 1, axis=1))
                    parts.append(f.reshape(blocks, GROUP, L))
                cols[phase, z, side] = jnp.concatenate(parts, axis=1).astype(LOW)

    small_lane = lax.broadcasted_iota(jnp.int32, (2 * GROUP, L), 1)
    ones = jnp.where(lax.broadcasted_iota(jnp.int32, (2 * GROUP, 2 * L), 0) < 3, 1.0, 0.0).astype(LOW)

    def live(k):
        z = base_ref[0] - 1 + k
        return jnp.where((z >= 0) & (z < slices), 1.0, 0.0).astype(FULL)

    first_live, last_live = live(0), live(window - 3)

    @pl.loop(0, blocks)
    def _(j):
        for phase in range(2):

            def gathered(k):
                return jnp.concatenate(
                    [cols[phase, k + a, b, j] for a in range(3) for b in range(3)], axis=0
                )

            hidden = []
            for k in range(2):
                patch = jnp.concatenate([gathered(2 * k), gathered(2 * k + 1)], axis=1)
                summed = matmul(one_ref[...], jnp.concatenate([patch, ones], axis=0))
                hidden.append(jnp.maximum(summed, 0.0))
            edge = [(hidden[0][:, :L] * first_live).astype(LOW), (hidden[1][:, L:] * last_live).astype(LOW)]
            inner = [hidden[0][:, L:].astype(LOW), hidden[1][:, :L].astype(LOW)]
            hidden = [
                jnp.concatenate([edge[0], inner[0]], axis=1),
                jnp.concatenate([inner[1], edge[1]], axis=1),
            ]
            width = 2 * GROUP
            middle = jnp.concatenate([inner[0], inner[1]], axis=1)
            terms = matmul(two_ref[...], jnp.concatenate([hidden[0], middle, hidden[1]], axis=0))
            for z in range(2):
                left, mid, right = [
                    terms[i * width : (i + 1) * width, z * L : (z + 1) * L] for i in range(3)
                ]
                left = jnp.where(small_lane == 0, 0.0, pltpu.roll(left, 1, axis=1))
                right = jnp.where(small_lane == L - 1, 0.0, pltpu.roll(right, L - 1, axis=1))
                both = left + mid + right
                for o in range(2):
                    acc[phase, z, o, j] = both[o * GROUP : (o + 1) * GROUP]

    for z in range(depth):
        for o in range(2):
            even = pltpu.roll(acc[0, z, o].reshape(R, L), R - 2, axis=0)
            odd = pltpu.roll(acc[1, z, o].reshape(R, L), 2, axis=0)
            noise = jnp.where(row >= R - 2, 0.0, even) + jnp.where(row < 2, 0.0, odd) + last_ref[o]
            est_ref[o, z] = jnp.transpose(field(o, z + 2) - noise)
            dual_ref[o, z] = jnp.transpose(noise)


def denoise(base, windows, one, bias, two, last):
    blocks, _, tall, L = windows[0].shape
    spread = tall * SETS // GROUP
    depth = spread - 4
    R = blocks * GROUP
    taps_one = one.reshape(3, 3, 3, 2, -1)
    taps_two = two.reshape(3, 3, 3, -1, 2)
    hid = taps_one.shape[-1]
    dx, rr, rb = jnp.arange(3), jnp.arange(GROUP), jnp.arange(STEP)
    into = (dx[:, None, None] == rr[None, :, None] - rb[None, None, :] - 1).astype(LOW)
    out = (dx[:, None, None] == rb[None, None, :] - rr[None, :, None] + 3).astype(LOW)
    first = einsum("abxio,xrk->koabir", taps_one, into).astype(LOW).reshape(STEP * hid, 18 * GROUP)
    second = einsum("abxoc,xrk->bcrako", taps_two, out).astype(LOW).reshape(6 * GROUP, 3 * STEP * hid)
    terms, left = [], jnp.tile(bias, STEP)
    for _ in range(3):
        terms.append(lax.reduce_precision(left, 8, 7))
        left = left - terms[-1]
    terms = jnp.stack(terms, axis=1).astype(LOW)
    first = jnp.concatenate([first, jnp.pad(terms, ((0, 0), (0, 2 * GROUP - 3)))], axis=1)
    shape = jax.ShapeDtypeStruct((2, depth, L, R), FULL)
    return pl.pallas_call(
        denoise_kernel,
        out_shape=(shape, shape),
        in_specs=[SMEM, VMEM, VMEM, VMEM, VMEM, SMEM],
        out_specs=(VMEM, VMEM),
        scratch_shapes=[
            pltpu.VMEM((2, spread, 3, blocks, 2 * GROUP, L), LOW),
            pltpu.VMEM((2, depth, 2, blocks, GROUP, L), FULL),
        ],
    )(base, *windows, first, second, last)


def on_device(
    kspace, coil_maps, sample_mask, tap_order, first_kernel, first_bias, second_kernel, second_bias
):
    n = lax.axis_size("slc")
    position = lax.axis_index("slc")
    _, depth, coils, H, W = coil_maps.shape
    slices, points = kspace.shape[1], kspace.shape[3]
    lines = points // W
    ncol = W // n

    fits = ncol == GROUP and coils * lines == W and coils % AT_ONCE == 0
    table_f, table_g = make_table(H, -1.0), make_table(H, 1.0)
    depth_f, depth_g = make_table(slices, -1.0), make_table(slices, 1.0)
    mask = sample_mask.astype(FULL).transpose(1, 0, 2)
    own_mask = lax.dynamic_slice_in_dim(sample_mask, position * lines, lines, axis=2)
    if fits:
        part = ncol // SETS
        place = position.astype(jnp.int32)[None]

        def send(blocks):
            got = list(blocks)
            for k in sorted(range(1, n), key=lambda k: abs(2 * k - n)):
                got[k] = lax.ppermute(blocks[k], "slc", [(i, (i + k) % n) for i in range(n)])
            return got

        maps = maps_step(place, coil_maps, n)
        maps = send(maps)
        own_mask = own_mask.transpose(0, 2, 1).reshape(slices, lines * coils).astype(FULL)
        table_x = make_table(W, 1.0).reshape(2 * W, 2 * W)
        depth_t = spread_table(depth_g, ncol).T
        depth_t = depth_t.reshape(-1, 2, slices, SETS, part).transpose(0, 3, 1, 2, 4).reshape(depth_t.shape)
        by_z = point_step(place, kspace, own_mask, low(table_x.T), low(depth_t), n)
        back_src = table_g.reshape(2, n, lines, 2 * H).transpose(1, 0, 2, 3).reshape(2 * H, 2 * H)
        tables = [
            low(table)
            for table in (
                back_src,
                table_f.reshape(2 * H, 2 * H),
                table_g.reshape(2 * H, 2 * H),
                spread_table(depth_f, part),
                spread_table(depth_g, part),
            )
        ]
        tall_mask = jnp.repeat(mask, part, axis=1)
        first = by_z[0]
        first = [swap(first)]
        later, tall_mask, maps = lax.optimization_barrier((by_z[1:], tall_mask, maps))
        later = send(later)
        windows = []
        for i, spectra in enumerate((first, later)):
            sent = data_step(i, n, place, maps, spectra, tall_mask, tables)
            if i == 0:
                _, later[:] = lax.optimization_barrier((sent, later))
            windows.append(swap(sent))
    else:
        maps = coil_maps.reshape(2, depth, coils, H, n, ncol).transpose(4, 2, 0, 1, 5, 3)
        maps = swap(maps)
        masked = kspace.reshape(2, slices, coils, lines, W) * own_mask.astype(LOW)[None, ..., None]
        by_x = einsum("pzcrj,pjqk->qzcrk", masked, low(make_table(W, 1.0))).astype(LOW)
        by_z = einsum("pjcrx,pjqk->xcqrk", by_x, low(depth_g)).astype(LOW)
        by_z = by_z.reshape(n, ncol, coils, 2 * lines, slices).transpose(0, 2, 3, 4, 1)
        spectra = swap(by_z.reshape(n, coils, 2 * lines, slices * ncol))
        got = swap(data_step_plain(maps, spectra, mask, *map(low, (table_f, table_g, depth_f, depth_g))))
        got = got.transpose(0, 3, 1, 2, 4).reshape(W // GROUP, SETS, GROUP // SETS, 2, depth + 4, H)
        got = got.transpose(1, 0, 3, 4, 2, 5).reshape(SETS, W // GROUP, 2, -1, H)
        windows = [got[i] for i in range(SETS)]

    kernel_one = tap_kernel(tap_order, first_kernel)
    kernel_two = tap_kernel(tap_order, second_kernel)
    base = jnp.stack([position * depth, jnp.int32(slices)]).astype(jnp.int32)
    return denoise(base, windows, kernel_one, first_bias, kernel_two, second_bias)


def solution(mesh):
    placed = (
        P("grp", None, None, "slc"),
        P("grp", "slc", None, None, None),
        P("grp", None, None),
        P(),
        P(),
        P(),
        P(),
        P(),
    )
    return jax.shard_map(
        on_device,
        mesh=mesh,
        in_specs=placed,
        out_specs=(P("grp", "slc", None, None), P("grp", "slc", None, None)),
        check_vma=False,
    )
```

```python
import functools
import math

import jax
import jax.numpy as jnp
import numpy as np
from jax import lax
from jax.experimental import pallas as pl
from jax.experimental.pallas import tpu as pltpu
from jax.sharding import PartitionSpec as P

GROUP = 8
STEP = 4
SETS = 2
AT_ONCE = 16
MAPS_AT_ONCE = 4
LOW = jnp.bfloat16
FULL = jnp.float32
VMEM = pl.BlockSpec(memory_space=pltpu.VMEM)
SMEM = pl.BlockSpec(memory_space=pltpu.SMEM)


def make_table(length, direction):
    positions = np.arange(length)
    angles = 2.0 * math.pi / length * (positions[:, None] * positions[None, :] % length)
    real_t = np.cos(angles) / math.sqrt(length)
    imag_t = direction * np.sin(angles) / math.sqrt(length)
    upper = np.stack([real_t, imag_t], axis=1)
    lower = np.stack([-imag_t, real_t], axis=1)
    return np.stack([upper, lower]).astype(np.float32)


def spread_table(table, copies):
    size = 2 * table.shape[1]
    return np.kron(table.reshape(size, size).T, np.eye(copies, dtype=np.float32))


def low(table):
    return jnp.asarray(table, LOW)


def tap_kernel(tap_order, stored):
    chosen = (tap_order[None, :] == jnp.arange(27, dtype=jnp.int32)[:, None]).astype(LOW)
    return einsum("tq,qio->tio", chosen, stored).astype(LOW)


def einsum(pattern, a, b):
    return jnp.einsum(pattern, a, b, preferred_element_type=FULL)


def swap(blocks):
    return lax.all_to_all(blocks, "slc", split_axis=0, concat_axis=0, tiled=True)


def matmul(a, b, dims=((1,), (0,))):
    return lax.dot_general(a, b, (dims, ((), ())), preferred_element_type=FULL)


def maps_kernel(place_ref, m_ref, *refs):
    _, depth, coils, H, W = m_ref.shape
    outs, scratch = refs[:-1], refs[-1]
    n = len(outs)
    part = W // (n * SETS)
    for c in range(coils):
        for p in range(2):
            turned = [
                jnp.transpose(m_ref[p, z, c]).astype(FULL).reshape(SETS, n // 2, 2 * part, H)
                for z in range(depth)
            ]
            for i in range(SETS):
                sides = [
                    jnp.concatenate([t[i, :, side * part : (side + 1) * part] for t in turned], axis=1)
                    for side in range(2)
                ]
                both = jnp.stack(sides, axis=1).reshape(n, depth * part, H)
                scratch[:, i, c, p] = both.astype(LOW)
    for k in range(n):
        outs[k][...] = scratch[lax.rem(place_ref[0] + k, n)]


def maps_step(place, coil_maps, n):
    _, depth, coils, H, W = coil_maps.shape
    rows = depth * W // (n * SETS)
    return pl.pallas_call(
        maps_kernel,
        grid=(coils // MAPS_AT_ONCE,),
        out_shape=[jax.ShapeDtypeStruct((SETS, coils, 2, rows, H), LOW)] * n,
        in_specs=[SMEM, pl.BlockSpec((2, depth, MAPS_AT_ONCE, H, W), lambda i: (0, 0, i, 0, 0))],
        out_specs=[pl.BlockSpec((SETS, MAPS_AT_ONCE, 2, rows, H), lambda i: (0, i, 0, 0, 0))] * n,
        scratch_shapes=[pltpu.VMEM((n, SETS, MAPS_AT_ONCE, 2, rows, H), LOW)],
    )(place, coil_maps)


def point_kernel(place_ref, k_ref, mask_ref, table_ref, depth_ref, *refs):
    _, slices, coils, _ = k_ref.shape
    whole, by_x, turned = refs[0], refs[-2], refs[-1]
    n, _, twice, _ = whole.shape
    lines = twice // 2
    W = table_ref.shape[0] // 2
    cols = W // n

    @pl.loop(0, slices)
    def _(z):
        rows = jnp.concatenate(
            [
                jnp.concatenate([k_ref[p, z, :, r * W : (r + 1) * W] for p in range(2)], axis=1)
                for r in range(lines)
            ],
            axis=0,
        )
        image = matmul(table_ref[...], rows, ((1,), (1,))) * mask_ref[pl.ds(z, 1), :]
        for p in range(2):
            by_x[:, p, z] = image[p * W : (p + 1) * W].reshape(n, cols, lines * coils)

    tiles, lane = turned.shape[1], turned.shape[3]
    each = tiles // SETS
    for k in range(n):
        d = lax.rem(place_ref[0] + k, n)
        own = by_x[d].reshape(2 * slices * cols, lines * coils).astype(LOW)
        full = matmul(own, depth_ref[...], ((0,), (0,)))
        for t in range(tiles):
            turned[k % 2, t] = full[:, t * lane : (t + 1) * lane]
        for c in range(coils):
            picked = [turned[k % 2, t, pl.ds(c, lines, stride=coils), :] for t in range(tiles)]
            for i in range(SETS):
                both = [
                    jnp.concatenate(picked[i * each + q * each // 2 :][: each // 2], axis=1)
                    for q in range(2)
                ]
                block = jnp.concatenate(both, axis=0).astype(LOW)
                if i == 0:
                    whole[d, c] = block
                else:
                    refs[1 + (i - 1) * n + k][c] = block


def point_step(place, kspace, mask, table, depth_table, n):
    _, slices, coils, points = kspace.shape
    W = table.shape[0] // 2
    lines, cols = points // W, W // n
    block = (coils, 2 * lines, slices * cols // SETS)
    return pl.pallas_call(
        point_kernel,
        out_shape=[jax.ShapeDtypeStruct((n, *block), LOW)] + [jax.ShapeDtypeStruct(block, LOW)] * (n * (SETS - 1)),
        in_specs=[SMEM] + [VMEM] * 4,
        out_specs=[VMEM] * (1 + n * (SETS - 1)),
        scratch_shapes=[
            pltpu.VMEM((n, 2, slices, cols, lines * coils), FULL),
            pltpu.VMEM((2, 2 * slices * cols // W, lines * coils, W), FULL),
        ],
    )(place, kspace, mask, table, depth_table)


def data_kernel(turn, n, place_ref, mask_ref, back_src, fwd, back, zf_ref, zb_ref, *refs):
    (out_ref, s_ref, ad_ref, sum_ref), sent = refs[-4:], refs[:-4]
    if len(sent) > n + 1:
        sent, u_ref = sent[:-1], sent[-1]
    _, coils, _, depth_cols, H = s_ref.shape
    rows = n * depth_cols
    for k in range(n):
        source = lax.rem(place_ref[0] + n - k, n)
        s_ref[source] = sent[k][turn]
        if len(sent) == 2 * n:
            u_ref[source] = sent[n + k][...]
    if len(sent) == n + 1:
        u_ref = sent[n]
    lines = u_ref.shape[2] // 2

    def sens(c):
        return [s_ref[:, c, p].astype(FULL).reshape(rows, H) for p in range(2)]

    def combine(total_ref, first, image):
        real, imag = total_ref[0], total_ref[1]
        for k in range(AT_ONCE):
            s = sens(first + k)
            r, i = image[k * rows : (k + 1) * rows, :H], image[k * rows : (k + 1) * rows, H:]
            real += s[0] * r + s[1] * i
            imag += s[0] * i - s[1] * r
        total_ref[0], total_ref[1] = real, imag

    ad_ref[...] = jnp.zeros_like(ad_ref)
    sum_ref[...] = jnp.zeros_like(sum_ref)

    @pl.loop(0, coils // AT_ONCE)
    def _(g):
        first = g * AT_ONCE
        u = [u_ref[:, first + k].reshape(n * 2 * lines, rows) for k in range(AT_ONCE)]
        combine(ad_ref, first, matmul(jnp.concatenate(u, axis=1), back_src[...], ((0,), (0,))))

    @pl.loop(0, coils // AT_ONCE)
    def _(g):
        first = g * AT_ONCE
        v = [ad_ref[0], ad_ref[1]]
        many = []
        for k in range(AT_ONCE):
            s = sens(first + k)
            both = [s[0] * v[0] - s[1] * v[1], s[0] * v[1] + s[1] * v[0]]
            many.append(jnp.concatenate(both, axis=1).astype(LOW))
        f = matmul(jnp.concatenate(many, axis=0), fwd[...]).astype(LOW)
        wide = []
        for k in range(AT_ONCE):
            part = f[k * rows : (k + 1) * rows]
            wide.append(jnp.concatenate([part[:, :H], part[:, H:]], axis=0))
        freq = matmul(zf_ref[...], jnp.concatenate(wide, axis=1))
        keep = []
        for k in range(AT_ONCE):
            part = freq[:, k * H : (k + 1) * H]
            m = mask_ref[first + k]
            keep.append(jnp.concatenate([part[:rows] * m, part[rows:] * m], axis=0))
        h = matmul(zb_ref[...], jnp.concatenate(keep, axis=1).astype(LOW)).astype(LOW)
        many = []
        for k in range(AT_ONCE):
            part = h[:, k * H : (k + 1) * H]
            many.append(jnp.concatenate([part[:rows], part[rows:]], axis=1))
        combine(sum_ref, first, matmul(jnp.concatenate(many, axis=0), back[...]))

    tall = out_ref.shape[2]
    edge = (tall - depth_cols) // 2
    for q in range(2):
        blank = jnp.zeros((edge, H), FULL)
        update = jnp.concatenate([blank, 2.0 * ad_ref[q] - sum_ref[q], blank], axis=0)
        for d in range(n):
            out_ref[d, q] = update[d * depth_cols : d * depth_cols + tall].astype(LOW)


def data_step(turn, n, place, maps, spectra, mask, tables):
    _, coils, _, depth_cols, H = maps[0].shape
    rows = n * depth_cols
    halo = 4 * (GROUP // SETS)
    scratch = [
        pltpu.VMEM((n, coils, 2, depth_cols, H), LOW),
        pltpu.VMEM((2, rows, H), FULL),
        pltpu.VMEM((2, rows, H), FULL),
    ]
    if len(spectra) == n:
        kernel = functools.partial(data_kernel_blocks, turn, n)
        scratch = scratch + [pltpu.VMEM((n, *spectra[0].shape), LOW)]
    else:
        kernel = functools.partial(data_kernel, turn, n)
    return pl.pallas_call(
        kernel,
        out_shape=jax.ShapeDtypeStruct((n, 2, depth_cols + halo, H), LOW),
        in_specs=[SMEM] + [VMEM] * (1 + len(tables) + n + len(spectra)),
        out_specs=VMEM,
        scratch_shapes=scratch,
    )(place, mask, *tables, *maps, *spectra)


def data_kernel_blocks(turn, n, *refs):
    data_kernel(turn, n, *refs[:-5], refs[-1], *refs[-5:-1])


def data_step_plain(maps, spectra, mask, table_f, table_g, depth_f, depth_g):
    n, coils, _, depth, cols, H = maps.shape
    slices = n * depth
    sens = maps.astype(FULL).transpose(2, 1, 4, 0, 3, 5).reshape(2, coils, cols, slices, H)
    part = spectra.reshape(n, coils, 2, H // n, slices, cols)
    part = part.transpose(2, 1, 5, 4, 0, 3).reshape(2, coils, cols, slices, H)

    def combine(image):
        return jnp.stack([
            jnp.sum(sens[0] * image[0] + sens[1] * image[1], axis=0),
            jnp.sum(sens[0] * image[1] - sens[1] * image[0], axis=0),
        ])

    v = combine(einsum("pcxzj,pjqk->qcxzk", part, table_g))
    w = jnp.stack([sens[0] * v[0] - sens[1] * v[1], sens[0] * v[1] + sens[1] * v[0]]).astype(LOW)
    f = einsum("pcxzj,pjqk->qcxzk", w, table_f).astype(LOW)
    g = einsum("pcxjk,pjqz->qcxzk", f, depth_f) * mask[:, None]
    h = einsum("pcxjk,pjqz->qcxzk", g.astype(LOW), depth_g).astype(LOW)
    update = 2.0 * v - combine(einsum("pcxzj,pjqk->qcxzk", h, table_g))
    padded = jnp.pad(update.astype(LOW), ((0, 0), (0, 0), (2, 2), (0, 0)))
    sent = jnp.stack([padded[:, :, d * depth : d * depth + depth + 4] for d in range(n)])
    return sent.transpose(0, 1, 3, 2, 4)


def gather_rows(refs, i, z, part):
    pieces = []
    for ref, skip in refs:
        count = ref.shape[0]
        pairs = ref[skip:, i].astype(FULL).reshape((count - skip) // 2, 2, *ref.shape[2:])
        sides = [pairs[:, side, z * part : (z + 1) * part] for side in range(2)]
        pieces.append(jnp.concatenate(sides, axis=1).reshape(-1, ref.shape[-1]))
    return jnp.concatenate(pieces, axis=0) if len(pieces) > 1 else pieces[0]


def hidden_blocks(base_ref, refs, one_ref, two_ref, acc, cols, start):
    part = GROUP // SETS
    window, blocks = cols.shape[1], cols.shape[3]
    L = cols.shape[-1]
    R = blocks * GROUP
    slices = base_ref[1]
    lane = lax.broadcasted_iota(jnp.int32, (R, L), 1)
    row = lax.broadcasted_iota(jnp.int32, (R, L), 0)

    for z in range(window):
        moved = ([], [])
        for i in range(2):
            f = gather_rows(refs, i, z, part)
            moved[0].append(jnp.where(row < 2, 0.0, pltpu.roll(f, 2, axis=0)))
            moved[1].append(jnp.where(row >= R - 2, 0.0, pltpu.roll(f, R - 2, axis=0)))
        for phase in range(2):
            for side in range(3):
                parts = []
                for f in moved[phase]:
                    if side == 0:
                        f = jnp.where(lane == 0, 0.0, pltpu.roll(f, 1, axis=1))
                    if side == 2:
                        f = jnp.where(lane == L - 1, 0.0, pltpu.roll(f, L - 1, axis=1))
                    parts.append(f.reshape(blocks, GROUP, L))
                cols[phase, z, side] = jnp.concatenate(parts, axis=1).astype(LOW)

    small_lane = lax.broadcasted_iota(jnp.int32, (2 * GROUP, L), 1)
    ones = jnp.where(lax.broadcasted_iota(jnp.int32, (2 * GROUP, 2 * L), 0) < 3, 1.0, 0.0).astype(LOW)

    def live(k):
        z = base_ref[0] - 1 + k
        return jnp.where((z >= 0) & (z < slices), 1.0, 0.0).astype(FULL)

    first_live, last_live = live(0), live(window - 3)

    @pl.loop(0, acc.shape[3])
    def _(j):
        for phase in range(2):

            def gathered(k):
                return jnp.concatenate(
                    [cols[phase, k + a, b, start + j] for a in range(3) for b in range(3)], axis=0
                )

            hidden = []
            for k in range(2):
                patch = jnp.concatenate([gathered(2 * k), gathered(2 * k + 1)], axis=1)
                summed = matmul(one_ref[...], jnp.concatenate([patch, ones], axis=0))
                hidden.append(jnp.maximum(summed, 0.0))
            edge = [(hidden[0][:, :L] * first_live).astype(LOW), (hidden[1][:, L:] * last_live).astype(LOW)]
            inner = [hidden[0][:, L:].astype(LOW), hidden[1][:, :L].astype(LOW)]
            stacked = [
                jnp.concatenate(pair, axis=1)
                for pair in ((edge[0], inner[0]), (inner[0], inner[1]), (inner[1], edge[1]))
            ]
            terms = matmul(two_ref[...], jnp.concatenate(stacked, axis=0))
            width = 2 * GROUP
            for z in range(2):
                left, mid, right = [
                    terms[i * width : (i + 1) * width, z * L : (z + 1) * L] for i in range(3)
                ]
                left = jnp.where(small_lane == 0, 0.0, pltpu.roll(left, 1, axis=1))
                right = jnp.where(small_lane == L - 1, 0.0, pltpu.roll(right, L - 1, axis=1))
                both = left + mid + right
                for o in range(2):
                    acc[phase, z, o, j] = both[o * GROUP : (o + 1) * GROUP]


def near_kernel(base_ref, wa_ref, one_ref, two_ref, acc, cols):
    hidden_blocks(base_ref, [(wa_ref, 0)], one_ref, two_ref, acc, cols, 0)


def far_kernel(base_ref, wa_ref, wb_ref, near_ref, one_ref, two_ref, last_ref, est_ref, dual_ref, cols, acc):
    part = GROUP // SETS
    overlap = cols.shape[3] * GROUP - wb_ref.shape[0] * part
    skip = wa_ref.shape[0] - overlap // part
    hidden_blocks(base_ref, [(wa_ref, skip), (wb_ref, 0)], one_ref, two_ref, acc, cols, cols.shape[3] - acc.shape[3])
    _, depth, L, R = est_ref.shape
    row = lax.broadcasted_iota(jnp.int32, (R, L), 0)
    for z in range(depth):
        for o in range(2):
            even, odd = [
                jnp.concatenate([ref[phase, z, o] for ref in (near_ref, acc)], axis=0).reshape(R, L)
                for phase in range(2)
            ]
            even = jnp.where(row >= R - 2, 0.0, pltpu.roll(even, R - 2, axis=0))
            odd = jnp.where(row < 2, 0.0, pltpu.roll(odd, 2, axis=0))
            noise = even + odd + last_ref[o]
            est_ref[o, z] = jnp.transpose(gather_rows([(wa_ref, 0), (wb_ref, 0)], o, z + 2, part) - noise)
            dual_ref[o, z] = jnp.transpose(noise)


def denoise_weights(one, bias, two):
    taps_one = one.reshape(3, 3, 3, 2, -1)
    taps_two = two.reshape(3, 3, 3, -1, 2)
    hid = taps_one.shape[-1]
    dx, rr, rb = jnp.arange(3), jnp.arange(GROUP), jnp.arange(STEP)
    into = (dx[:, None, None] == rr[None, :, None] - rb[None, None, :] - 1).astype(LOW)
    out = (dx[:, None, None] == rb[None, None, :] - rr[None, :, None] + 3).astype(LOW)
    first = einsum("abxio,xrk->koabir", taps_one, into).astype(LOW).reshape(STEP * hid, 18 * GROUP)
    second = einsum("abxoc,xrk->bcrako", taps_two, out).astype(LOW).reshape(6 * GROUP, 3 * STEP * hid)
    terms, left = [], jnp.tile(bias, STEP)
    for _ in range(3):
        terms.append(lax.reduce_precision(left, 8, 7))
        left = left - terms[-1]
    terms = jnp.stack(terms, axis=1).astype(LOW)
    first = jnp.concatenate([first, jnp.pad(terms, ((0, 0), (0, 2 * GROUP - 3)))], axis=1)
    return first, second


def denoise_near(base, window, first, second):
    count, _, tall, L = window.shape
    spread = tall * SETS // GROUP
    blocks = count * GROUP // SETS // GROUP
    return pl.pallas_call(
        near_kernel,
        out_shape=jax.ShapeDtypeStruct((2, spread - 4, 2, blocks - 1, GROUP, L), FULL),
        in_specs=[SMEM, VMEM, VMEM, VMEM],
        out_specs=VMEM,
        scratch_shapes=[pltpu.VMEM((2, spread, 3, blocks, 2 * GROUP, L), LOW)],
    )(base, window, first, second)


def denoise_far(base, windows, near, first, second, last):
    count, _, tall, L = windows[0].shape
    spread = tall * SETS // GROUP
    depth = spread - 4
    half = count * GROUP // SETS // GROUP
    shape = jax.ShapeDtypeStruct((2, depth, L, 2 * half * GROUP), FULL)
    return pl.pallas_call(
        far_kernel,
        out_shape=(shape, shape),
        in_specs=[SMEM] + [VMEM] * 5 + [SMEM],
        out_specs=(VMEM, VMEM),
        scratch_shapes=[
            pltpu.VMEM((2, spread, 3, half + 2, 2 * GROUP, L), LOW),
            pltpu.VMEM((2, depth, 2, half + 1, GROUP, L), FULL),
        ],
    )(base, *windows, near, first, second, last)


def on_device(
    kspace, coil_maps, sample_mask, tap_order, first_kernel, first_bias, second_kernel, second_bias
):
    n = lax.axis_size("slc")
    position = lax.axis_index("slc")
    _, depth, coils, H, W = coil_maps.shape
    slices, points = kspace.shape[1], kspace.shape[3]
    lines = points // W
    ncol = W // n

    base = jnp.stack([position * depth, jnp.int32(slices)]).astype(jnp.int32)
    weights = denoise_weights(
        tap_kernel(tap_order, first_kernel), first_bias, tap_kernel(tap_order, second_kernel)
    )
    fits = ncol == GROUP and coils * lines == W and coils % AT_ONCE == 0
    table_f, table_g = make_table(H, -1.0), make_table(H, 1.0)
    depth_f, depth_g = make_table(slices, -1.0), make_table(slices, 1.0)
    mask = sample_mask.astype(FULL).transpose(1, 0, 2)
    own_mask = lax.dynamic_slice_in_dim(sample_mask, position * lines, lines, axis=2)
    if fits:
        part = ncol // SETS
        place = position.astype(jnp.int32)[None]

        order = sorted(range(1, n), key=lambda k: abs(2 * k - n))

        def send(blocks):
            got = list(blocks)
            for k in order:
                got[k] = lax.ppermute(blocks[k], "slc", [(i, (i + k) % n) for i in range(n)])
            return got

        maps = maps_step(place, coil_maps, n)
        maps = send(maps)
        own_mask = own_mask.transpose(0, 2, 1).reshape(slices, lines * coils).astype(FULL)
        table_rows = make_table(W, 1.0).reshape(2 * W, 2, SETS, n, part)
        table_rows = table_rows.transpose(1, 3, 2, 4, 0).reshape(2 * W, 2 * W)
        depth_t = spread_table(depth_g, ncol).T
        depth_t = depth_t.reshape(-1, 2, slices, SETS, part).transpose(0, 3, 1, 2, 4).reshape(depth_t.shape)
        by_z = point_step(place, kspace, own_mask, low(table_rows), low(depth_t), n)
        back_src = table_g.reshape(2, n, lines, 2 * H).transpose(1, 0, 2, 3).reshape(2 * H, 2 * H)
        tables = [
            low(table)
            for table in (
                back_src,
                table_f.reshape(2 * H, 2 * H),
                table_g.reshape(2 * H, 2 * H),
                spread_table(depth_f, part),
                spread_table(depth_g, part),
            )
        ]
        tall_mask = jnp.repeat(mask, part, axis=1)
        first = by_z[0]
        first = [swap(first)]
        held = [maps[k] for k in order[: n - 3]]
        later, tall_mask, held, base, weights = lax.optimization_barrier(
            (by_z[1:], tall_mask, held, base, weights)
        )
        for k, block in zip(order[: n - 3], held):
            maps[k] = block
        later = send(later)
        windows = []
        for i, spectra in enumerate((first, later)):
            sent = data_step(i, n, place, maps, spectra, tall_mask, tables)
            if i == 0:
                _, later[:] = lax.optimization_barrier((sent, later))
            windows.append(swap(sent))
    else:
        maps = coil_maps.reshape(2, depth, coils, H, n, ncol).transpose(4, 2, 0, 1, 5, 3)
        maps = swap(maps)
        masked = kspace.reshape(2, slices, coils, lines, W) * own_mask.astype(LOW)[None, ..., None]
        by_x = einsum("pzcrj,pjqk->qzcrk", masked, low(make_table(W, 1.0))).astype(LOW)
        by_z = einsum("pjcrx,pjqk->xcqrk", by_x, low(depth_g)).astype(LOW)
        by_z = by_z.reshape(n, ncol, coils, 2 * lines, slices).transpose(0, 2, 3, 4, 1)
        spectra = swap(by_z.reshape(n, coils, 2 * lines, slices * ncol))
        got = swap(data_step_plain(maps, spectra, mask, *map(low, (table_f, table_g, depth_f, depth_g))))
        part = GROUP // SETS
        got = got.transpose(0, 3, 1, 2, 4).reshape(SETS, W // GROUP, part, 2, depth + 4, H)
        got = got.transpose(0, 1, 3, 4, 2, 5).reshape(SETS, W // GROUP, 2, -1, H)
        windows = [got[i] for i in range(SETS)]

    near = denoise_near(base, windows[0], *weights)
    return denoise_far(base, windows, near, *weights, second_bias)


def solution(mesh):
    placed = (
        P("grp", None, None, "slc"),
        P("grp", "slc", None, None, None),
        P("grp", None, None),
        P(),
        P(),
        P(),
        P(),
        P(),
    )
    return jax.shard_map(
        on_device,
        mesh=mesh,
        in_specs=placed,
        out_specs=(P("grp", "slc", None, None), P("grp", "slc", None, None)),
        check_vma=False,
    )
```

```python
import functools
import math

import jax
import jax.numpy as jnp
import numpy as np
from jax import lax
from jax.experimental import pallas as pl
from jax.experimental.pallas import tpu as pltpu
from jax.sharding import PartitionSpec as P

GROUP = 8
STEP = 4
SETS = 2
AT_ONCE = 16
MAPS_AT_ONCE = 8
LOW = jnp.bfloat16
FULL = jnp.float32
VMEM = pl.BlockSpec(memory_space=pltpu.VMEM)
SMEM = pl.BlockSpec(memory_space=pltpu.SMEM)


def make_table(length, direction):
    positions = np.arange(length)
    angles = 2.0 * math.pi / length * (positions[:, None] * positions[None, :] % length)
    real_t = np.cos(angles) / math.sqrt(length)
    imag_t = direction * np.sin(angles) / math.sqrt(length)
    upper = np.stack([real_t, imag_t], axis=1)
    lower = np.stack([-imag_t, real_t], axis=1)
    return np.stack([upper, lower]).astype(np.float32)


def spread_table(table, copies):
    size = 2 * table.shape[1]
    return np.kron(table.reshape(size, size).T, np.eye(copies, dtype=np.float32))


def low(table):
    return jnp.asarray(table, LOW)


def tap_kernel(tap_order, stored):
    chosen = (tap_order[None, :] == jnp.arange(27, dtype=jnp.int32)[:, None]).astype(LOW)
    return einsum("tq,qio->tio", chosen, stored).astype(LOW)


def einsum(pattern, a, b):
    return jnp.einsum(pattern, a, b, preferred_element_type=FULL)


def swap(blocks):
    return lax.all_to_all(blocks, "slc", split_axis=0, concat_axis=0, tiled=True)


def matmul(a, b, dims=((1,), (0,))):
    return lax.dot_general(a, b, (dims, ((), ())), preferred_element_type=FULL)


def maps_kernel(place_ref, m_ref, *refs):
    _, depth, coils, H, W = m_ref.shape
    outs, scratch = refs[:-1], refs[-1]
    n = len(outs)
    part = W // (n * SETS)
    for c in range(coils):
        for p in range(2):
            turned = [
                jnp.transpose(m_ref[p, z, c]).astype(FULL).reshape(SETS, n // 2, 2 * part, H)
                for z in range(depth)
            ]
            for i in range(SETS):
                sides = [
                    jnp.concatenate([t[i, :, side * part : (side + 1) * part] for t in turned], axis=1)
                    for side in range(2)
                ]
                both = jnp.stack(sides, axis=1).reshape(n, depth * part, H)
                scratch[:, i, c, p] = both.astype(LOW)
    for k in range(n):
        outs[k][...] = scratch[lax.rem(place_ref[0] + k, n)]


def maps_step(place, coil_maps, n):
    _, depth, coils, H, W = coil_maps.shape
    rows = depth * W // (n * SETS)
    return pl.pallas_call(
        maps_kernel,
        grid=(coils // MAPS_AT_ONCE,),
        out_shape=[jax.ShapeDtypeStruct((SETS, coils, 2, rows, H), LOW)] * n,
        in_specs=[SMEM, pl.BlockSpec((2, depth, MAPS_AT_ONCE, H, W), lambda i: (0, 0, i, 0, 0))],
        out_specs=[pl.BlockSpec((SETS, MAPS_AT_ONCE, 2, rows, H), lambda i: (0, i, 0, 0, 0))] * n,
        scratch_shapes=[pltpu.VMEM((n, SETS, MAPS_AT_ONCE, 2, rows, H), LOW)],
    )(place, coil_maps)


def point_kernel(place_ref, k_ref, mask_ref, table_ref, depth_ref, *refs):
    _, slices, coils, _ = k_ref.shape
    whole, by_x, turned = refs[0], refs[-2], refs[-1]
    n, _, twice, _ = whole.shape
    lines = twice // 2
    W = table_ref.shape[0] // 2
    cols = W // n

    @pl.loop(0, slices)
    def _(z):
        rows = jnp.concatenate(
            [
                jnp.concatenate([k_ref[p, z, :, r * W : (r + 1) * W] for p in range(2)], axis=1)
                for r in range(lines)
            ],
            axis=0,
        )
        image = matmul(table_ref[...], rows, ((1,), (1,))) * mask_ref[pl.ds(z, 1), :]
        for p in range(2):
            by_x[:, p, z] = image[p * W : (p + 1) * W].reshape(n, cols, lines * coils)

    tiles, lane = turned.shape[1], turned.shape[3]
    each = tiles // SETS
    for k in range(n):
        d = lax.rem(place_ref[0] + k, n)
        own = by_x[d].reshape(2 * slices * cols, lines * coils).astype(LOW)
        full = matmul(own, depth_ref[...], ((0,), (0,)))
        for t in range(tiles):
            turned[k % 2, t] = full[:, t * lane : (t + 1) * lane]
        for c in range(coils):
            picked = [turned[k % 2, t, pl.ds(c, lines, stride=coils), :] for t in range(tiles)]
            for i in range(SETS):
                both = [
                    jnp.concatenate(picked[i * each + q * each // 2 :][: each // 2], axis=1)
                    for q in range(2)
                ]
                block = jnp.concatenate(both, axis=0).astype(LOW)
                if i == 0:
                    whole[d, c] = block
                else:
                    refs[1 + (i - 1) * n + k][c] = block


def point_step(place, kspace, mask, table, depth_table, n):
    _, slices, coils, points = kspace.shape
    W = table.shape[0] // 2
    lines, cols = points // W, W // n
    block = (coils, 2 * lines, slices * cols // SETS)
    return pl.pallas_call(
        point_kernel,
        out_shape=[jax.ShapeDtypeStruct((n, *block), LOW)] + [jax.ShapeDtypeStruct(block, LOW)] * (n * (SETS - 1)),
        in_specs=[SMEM] + [VMEM] * 4,
        out_specs=[VMEM] * (1 + n * (SETS - 1)),
        scratch_shapes=[
            pltpu.VMEM((n, 2, slices, cols, lines * coils), FULL),
            pltpu.VMEM((2, 2 * slices * cols // W, lines * coils, W), FULL),
        ],
    )(place, kspace, mask, table, depth_table)


def data_kernel(turn, n, place_ref, *refs):
    count = len(refs) - 12
    held, blocks, out_ref = refs[:6], refs[6:count], refs[count]
    ad_ref, sum_ref, s_ref, u_ref, *placed, sems = refs[count + 1 :]
    mask_ref, back_src, fwd, back, zf_ref, zb_ref = placed
    _, coils, _, depth_cols, H = s_ref.shape
    rows = n * depth_cols
    lines = u_ref.shape[2] // 2

    moves = [(held[1], back_src)]
    for k in range(n):
        source = lax.rem(place_ref[0] + n - k, n)
        moves.append((blocks[k].at[turn], s_ref.at[source]))
        if len(blocks) == 2 * n:
            moves.append((blocks[n + k], u_ref.at[source]))
    if len(blocks) == n + 1:
        moves.append((blocks[n], u_ref))
    early = len(moves)
    moves += [(held[i], placed[i]) for i in (2, 4, 0, 5, 3)]
    copies = [pltpu.make_async_copy(source, place, sems.at[i]) for i, (source, place) in enumerate(moves)]
    for copy in copies:
        copy.start()

    def sens(c):
        return [s_ref[:, c, p].astype(FULL).reshape(rows, H) for p in range(2)]

    def combine(total_ref, first, image):
        real, imag = total_ref[0], total_ref[1]
        for k in range(AT_ONCE):
            s = sens(first + k)
            r, i = image[k * rows : (k + 1) * rows, :H], image[k * rows : (k + 1) * rows, H:]
            real += s[0] * r + s[1] * i
            imag += s[0] * i - s[1] * r
        total_ref[0], total_ref[1] = real, imag

    ad_ref[...] = jnp.zeros_like(ad_ref)
    sum_ref[...] = jnp.zeros_like(sum_ref)
    for copy in copies[:early]:
        copy.wait()

    @pl.loop(0, coils // AT_ONCE)
    def _(g):
        first = g * AT_ONCE
        u = [u_ref[:, first + k].reshape(n * 2 * lines, rows) for k in range(AT_ONCE)]
        combine(ad_ref, first, matmul(jnp.concatenate(u, axis=1), back_src[...], ((0,), (0,))))

    for copy in copies[early:]:
        copy.wait()

    @pl.loop(0, coils // AT_ONCE)
    def _(g):
        first = g * AT_ONCE
        v = [ad_ref[0], ad_ref[1]]
        many = []
        for k in range(AT_ONCE):
            s = sens(first + k)
            both = [s[0] * v[0] - s[1] * v[1], s[0] * v[1] + s[1] * v[0]]
            many.append(jnp.concatenate(both, axis=1).astype(LOW))
        f = matmul(jnp.concatenate(many, axis=0), fwd[...]).astype(LOW)
        wide = []
        for k in range(AT_ONCE):
            part = f[k * rows : (k + 1) * rows]
            wide.append(jnp.concatenate([part[:, :H], part[:, H:]], axis=0))
        freq = matmul(zf_ref[...], jnp.concatenate(wide, axis=1))
        keep = []
        for k in range(AT_ONCE):
            part = freq[:, k * H : (k + 1) * H]
            m = mask_ref[first + k]
            keep.append(jnp.concatenate([part[:rows] * m, part[rows:] * m], axis=0))
        h = matmul(zb_ref[...], jnp.concatenate(keep, axis=1).astype(LOW)).astype(LOW)
        many = []
        for k in range(AT_ONCE):
            part = h[:, k * H : (k + 1) * H]
            many.append(jnp.concatenate([part[:rows], part[rows:]], axis=1))
        combine(sum_ref, first, matmul(jnp.concatenate(many, axis=0), back[...]))

    tall = out_ref.shape[2]
    edge = (tall - depth_cols) // 2
    for q in range(2):
        blank = jnp.zeros((edge, H), FULL)
        update = jnp.concatenate([blank, 2.0 * ad_ref[q] - sum_ref[q], blank], axis=0)
        for d in range(n):
            out_ref[d, q] = update[d * depth_cols : d * depth_cols + tall].astype(LOW)


def data_step(turn, n, place, maps, spectra, mask, tables):
    _, coils, _, depth_cols, H = maps[0].shape
    rows = n * depth_cols
    halo = 4 * (GROUP // SETS)
    held = [mask, *tables]
    block = spectra[0].shape[-3:]
    return pl.pallas_call(
        functools.partial(data_kernel, turn, n),
        out_shape=jax.ShapeDtypeStruct((n, 2, depth_cols + halo, H), LOW),
        in_specs=[SMEM] + [pl.BlockSpec(memory_space=pl.ANY)] * (len(held) + n + len(spectra)),
        out_specs=VMEM,
        scratch_shapes=[
            pltpu.VMEM((2, rows, H), FULL),
            pltpu.VMEM((2, rows, H), FULL),
            pltpu.VMEM((n, coils, 2, depth_cols, H), LOW),
            pltpu.VMEM((n, *block), LOW),
            *[pltpu.VMEM(array.shape, array.dtype) for array in held],
            pltpu.SemaphoreType.DMA((len(held) + n + len(spectra),)),
        ],
    )(place, *held, *maps, *spectra)


def data_step_plain(maps, spectra, mask, table_f, table_g, depth_f, depth_g):
    n, coils, _, depth, cols, H = maps.shape
    slices = n * depth
    sens = maps.astype(FULL).transpose(2, 1, 4, 0, 3, 5).reshape(2, coils, cols, slices, H)
    part = spectra.reshape(n, coils, 2, H // n, slices, cols)
    part = part.transpose(2, 1, 5, 4, 0, 3).reshape(2, coils, cols, slices, H)

    def combine(image):
        return jnp.stack([
            jnp.sum(sens[0] * image[0] + sens[1] * image[1], axis=0),
            jnp.sum(sens[0] * image[1] - sens[1] * image[0], axis=0),
        ])

    v = combine(einsum("pcxzj,pjqk->qcxzk", part, table_g))
    w = jnp.stack([sens[0] * v[0] - sens[1] * v[1], sens[0] * v[1] + sens[1] * v[0]]).astype(LOW)
    f = einsum("pcxzj,pjqk->qcxzk", w, table_f).astype(LOW)
    g = einsum("pcxjk,pjqz->qcxzk", f, depth_f) * mask[:, None]
    h = einsum("pcxjk,pjqz->qcxzk", g.astype(LOW), depth_g).astype(LOW)
    update = 2.0 * v - combine(einsum("pcxzj,pjqk->qcxzk", h, table_g))
    padded = jnp.pad(update.astype(LOW), ((0, 0), (0, 0), (2, 2), (0, 0)))
    sent = jnp.stack([padded[:, :, d * depth : d * depth + depth + 4] for d in range(n)])
    return sent.transpose(0, 1, 3, 2, 4)


def gather_rows(refs, i, z, part):
    pieces = []
    for ref, skip in refs:
        count = ref.shape[0]
        pairs = ref[skip:, i].astype(FULL).reshape((count - skip) // 2, 2, *ref.shape[2:])
        sides = [pairs[:, side, z * part : (z + 1) * part] for side in range(2)]
        pieces.append(jnp.concatenate(sides, axis=1).reshape(-1, ref.shape[-1]))
    return jnp.concatenate(pieces, axis=0) if len(pieces) > 1 else pieces[0]


def hidden_blocks(base_ref, refs, one_ref, two_ref, acc, cols, start):
    part = GROUP // SETS
    window, blocks = cols.shape[1], cols.shape[3]
    L = cols.shape[-1]
    R = blocks * GROUP
    slices = base_ref[1]
    lane = lax.broadcasted_iota(jnp.int32, (R, L), 1)
    row = lax.broadcasted_iota(jnp.int32, (R, L), 0)

    for z in range(window):
        moved = ([], [])
        for i in range(2):
            f = gather_rows(refs, i, z, part)
            moved[0].append(jnp.where(row < 2, 0.0, pltpu.roll(f, 2, axis=0)))
            moved[1].append(jnp.where(row >= R - 2, 0.0, pltpu.roll(f, R - 2, axis=0)))
        for phase in range(2):
            for side in range(3):
                parts = []
                for f in moved[phase]:
                    if side == 0:
                        f = jnp.where(lane == 0, 0.0, pltpu.roll(f, 1, axis=1))
                    if side == 2:
                        f = jnp.where(lane == L - 1, 0.0, pltpu.roll(f, L - 1, axis=1))
                    parts.append(f.reshape(blocks, GROUP, L))
                cols[phase, z, side] = jnp.concatenate(parts, axis=1).astype(LOW)

    small_lane = lax.broadcasted_iota(jnp.int32, (2 * GROUP, L), 1)
    ones = jnp.where(lax.broadcasted_iota(jnp.int32, (2 * GROUP, 2 * L), 0) < 3, 1.0, 0.0).astype(LOW)

    def live(k):
        z = base_ref[0] - 1 + k
        return jnp.where((z >= 0) & (z < slices), 1.0, 0.0).astype(FULL)

    first_live, last_live = live(0), live(window - 3)

    @pl.loop(0, acc.shape[3])
    def _(j):
        for phase in range(2):

            def gathered(k):
                return jnp.concatenate(
                    [cols[phase, k + a, b, start + j] for a in range(3) for b in range(3)], axis=0
                )

            hidden = []
            for k in range(2):
                patch = jnp.concatenate([gathered(2 * k), gathered(2 * k + 1)], axis=1)
                summed = matmul(one_ref[...], jnp.concatenate([patch, ones], axis=0))
                hidden.append(jnp.maximum(summed, 0.0))
            edge = [(hidden[0][:, :L] * first_live).astype(LOW), (hidden[1][:, L:] * last_live).astype(LOW)]
            inner = [hidden[0][:, L:].astype(LOW), hidden[1][:, :L].astype(LOW)]
            stacked = [
                jnp.concatenate(pair, axis=1)
                for pair in ((edge[0], inner[0]), (inner[0], inner[1]), (inner[1], edge[1]))
            ]
            terms = matmul(two_ref[...], jnp.concatenate(stacked, axis=0))
            width = 2 * GROUP
            for z in range(2):
                left, mid, right = [
                    terms[i * width : (i + 1) * width, z * L : (z + 1) * L] for i in range(3)
                ]
                left = jnp.where(small_lane == 0, 0.0, pltpu.roll(left, 1, axis=1))
                right = jnp.where(small_lane == L - 1, 0.0, pltpu.roll(right, L - 1, axis=1))
                both = left + mid + right
                for o in range(2):
                    acc[phase, z, o, j] = both[o * GROUP : (o + 1) * GROUP]


def near_kernel(base_ref, wa_ref, one_ref, two_ref, acc, cols):
    hidden_blocks(base_ref, [(wa_ref, 0)], one_ref, two_ref, acc, cols, 0)


def far_kernel(base_ref, wa_ref, wb_ref, near_ref, one_ref, two_ref, last_ref, est_ref, dual_ref, cols, acc):
    part = GROUP // SETS
    overlap = cols.shape[3] * GROUP - wb_ref.shape[0] * part
    skip = wa_ref.shape[0] - overlap // part
    hidden_blocks(base_ref, [(wa_ref, skip), (wb_ref, 0)], one_ref, two_ref, acc, cols, cols.shape[3] - acc.shape[3])
    _, depth, L, R = est_ref.shape
    row = lax.broadcasted_iota(jnp.int32, (R, L), 0)
    for z in range(depth):
        for o in range(2):
            even, odd = [
                jnp.concatenate([ref[phase, z, o] for ref in (near_ref, acc)], axis=0).reshape(R, L)
                for phase in range(2)
            ]
            even = jnp.where(row >= R - 2, 0.0, pltpu.roll(even, R - 2, axis=0))
            odd = jnp.where(row < 2, 0.0, pltpu.roll(odd, 2, axis=0))
            noise = even + odd + last_ref[o]
            est_ref[o, z] = jnp.transpose(gather_rows([(wa_ref, 0), (wb_ref, 0)], o, z + 2, part) - noise)
            dual_ref[o, z] = jnp.transpose(noise)


def denoise_weights(one, bias, two):
    taps_one = one.reshape(3, 3, 3, 2, -1)
    taps_two = two.reshape(3, 3, 3, -1, 2)
    hid = taps_one.shape[-1]
    dx, rr, rb = jnp.arange(3), jnp.arange(GROUP), jnp.arange(STEP)
    into = (dx[:, None, None] == rr[None, :, None] - rb[None, None, :] - 1).astype(LOW)
    out = (dx[:, None, None] == rb[None, None, :] - rr[None, :, None] + 3).astype(LOW)
    first = einsum("abxio,xrk->koabir", taps_one, into).astype(LOW).reshape(STEP * hid, 18 * GROUP)
    second = einsum("abxoc,xrk->bcrako", taps_two, out).astype(LOW).reshape(6 * GROUP, 3 * STEP * hid)
    terms, left = [], jnp.tile(bias, STEP)
    for _ in range(3):
        terms.append(lax.reduce_precision(left, 8, 7))
        left = left - terms[-1]
    terms = jnp.stack(terms, axis=1).astype(LOW)
    first = jnp.concatenate([first, jnp.pad(terms, ((0, 0), (0, 2 * GROUP - 3)))], axis=1)
    return first, second


def denoise_near(base, window, first, second):
    count, _, tall, L = window.shape
    spread = tall * SETS // GROUP
    blocks = count * GROUP // SETS // GROUP
    return pl.pallas_call(
        near_kernel,
        out_shape=jax.ShapeDtypeStruct((2, spread - 4, 2, blocks - 1, GROUP, L), FULL),
        in_specs=[SMEM, VMEM, VMEM, VMEM],
        out_specs=VMEM,
        scratch_shapes=[pltpu.VMEM((2, spread, 3, blocks, 2 * GROUP, L), LOW)],
    )(base, pltpu.with_memory_space_constraint(window, pltpu.VMEM), first, second)


def denoise_far(base, windows, near, first, second, last):
    count, _, tall, L = windows[0].shape
    spread = tall * SETS // GROUP
    depth = spread - 4
    half = count * GROUP // SETS // GROUP
    shape = jax.ShapeDtypeStruct((2, depth, L, 2 * half * GROUP), FULL)
    return pl.pallas_call(
        far_kernel,
        out_shape=(shape, shape),
        in_specs=[SMEM] + [VMEM] * 5 + [SMEM],
        out_specs=(VMEM, VMEM),
        scratch_shapes=[
            pltpu.VMEM((2, spread, 3, half + 2, 2 * GROUP, L), LOW),
            pltpu.VMEM((2, depth, 2, half + 1, GROUP, L), FULL),
        ],
    )(base, *[pltpu.with_memory_space_constraint(w, pltpu.VMEM) for w in windows], near, first, second, last)


def on_device(
    kspace, coil_maps, sample_mask, tap_order, first_kernel, first_bias, second_kernel, second_bias
):
    n = lax.axis_size("slc")
    position = lax.axis_index("slc")
    _, depth, coils, H, W = coil_maps.shape
    slices, points = kspace.shape[1], kspace.shape[3]
    lines = points // W
    ncol = W // n

    base = jnp.stack([position * depth, jnp.int32(slices)]).astype(jnp.int32)
    weights = denoise_weights(
        tap_kernel(tap_order, first_kernel), first_bias, tap_kernel(tap_order, second_kernel)
    )
    fits = ncol == GROUP and coils * lines == W and coils % AT_ONCE == 0
    table_f, table_g = make_table(H, -1.0), make_table(H, 1.0)
    depth_f, depth_g = make_table(slices, -1.0), make_table(slices, 1.0)
    mask = sample_mask.astype(FULL).transpose(1, 0, 2)
    own_mask = lax.dynamic_slice_in_dim(sample_mask, position * lines, lines, axis=2)
    if fits:
        part = ncol // SETS
        place = position.astype(jnp.int32)[None]

        order = sorted(range(1, n), key=lambda k: abs(2 * k - n))

        def send(blocks, turns):
            got = list(blocks)
            for k in turns:
                got[k] = lax.ppermute(blocks[k], "slc", [(i, (i + k) % n) for i in range(n)])
            return got

        maps = maps_step(place, coil_maps, n)
        soon, rest = order[:8], order[8:]
        maps = send(maps, soon)
        own_mask = own_mask.transpose(0, 2, 1).reshape(slices, lines * coils).astype(FULL)
        table_rows = make_table(W, 1.0).reshape(2 * W, 2, SETS, n, part)
        table_rows = table_rows.transpose(1, 3, 2, 4, 0).reshape(2 * W, 2 * W)
        depth_t = spread_table(depth_g, ncol).T
        depth_t = depth_t.reshape(-1, 2, slices, SETS, part).transpose(0, 3, 1, 2, 4).reshape(depth_t.shape)
        by_z = point_step(place, kspace, own_mask, low(table_rows), low(depth_t), n)
        back_src = table_g.reshape(2, n, lines, 2 * H).transpose(1, 0, 2, 3).reshape(2 * H, 2 * H)
        tables = [
            low(table)
            for table in (
                back_src,
                table_f.reshape(2 * H, 2 * H),
                table_g.reshape(2 * H, 2 * H),
                spread_table(depth_f, part),
                spread_table(depth_g, part),
            )
        ]
        tall_mask = jnp.repeat(mask, part, axis=1)
        first = by_z[0]
        first = [swap(first)]
        maps = send(maps, rest)
        held = [maps[k] for k in soon]
        later, tall_mask, held, base, weights = lax.optimization_barrier(
            (by_z[1:], tall_mask, held, base, weights)
        )
        for k, block in zip(soon, held):
            maps[k] = block
        later = send(later, range(1, n))
        windows = []
        for i, spectra in enumerate((first, later)):
            sent = data_step(i, n, place, maps, spectra, tall_mask, tables)
            if i == 0:
                _, later[:] = lax.optimization_barrier((sent, later))
            windows.append(swap(sent))
    else:
        maps = coil_maps.reshape(2, depth, coils, H, n, ncol).transpose(4, 2, 0, 1, 5, 3)
        maps = swap(maps)
        masked = kspace.reshape(2, slices, coils, lines, W) * own_mask.astype(LOW)[None, ..., None]
        by_x = einsum("pzcrj,pjqk->qzcrk", masked, low(make_table(W, 1.0))).astype(LOW)
        by_z = einsum("pjcrx,pjqk->xcqrk", by_x, low(depth_g)).astype(LOW)
        by_z = by_z.reshape(n, ncol, coils, 2 * lines, slices).transpose(0, 2, 3, 4, 1)
        spectra = swap(by_z.reshape(n, coils, 2 * lines, slices * ncol))
        got = swap(data_step_plain(maps, spectra, mask, *map(low, (table_f, table_g, depth_f, depth_g))))
        part = GROUP // SETS
        got = got.transpose(0, 3, 1, 2, 4).reshape(SETS, W // GROUP, part, 2, depth + 4, H)
        got = got.transpose(0, 1, 3, 4, 2, 5).reshape(SETS, W // GROUP, 2, -1, H)
        windows = [got[i] for i in range(SETS)]

    near = denoise_near(base, windows[0], *weights)
    return denoise_far(base, windows, near, *weights, second_bias)


def solution(mesh):
    placed = (
        P("grp", None, None, "slc"),
        P("grp", "slc", None, None, None),
        P("grp", None, None),
        P(),
        P(),
        P(),
        P(),
        P(),
    )
    return jax.shard_map(
        on_device,
        mesh=mesh,
        in_specs=placed,
        out_specs=(P("grp", "slc", None, None), P("grp", "slc", None, None)),
        check_vma=False,
    )
```
